32 devices in a mesh: row: 4 (over y, x), col: 8 (over z, core).
Axes of the slice: x: 2, y: 2, z: 4, core: 2. Of those that a mesh axis runs over, the one named last changes fastest.
Arguments:
- tokens: bfloat16 [294912, 1024], P(('row', 'col')), may hold values from -6 to 6
- router_weight: bfloat16 [1024], P(('row', 'col')), may hold values from -0.1875 to 0.1875
- norm_first: bfloat16 [1024], P(('row', 'col')), may hold values from 0.099609375 to 1.8984375
- qkv_weight: bfloat16 [1024, 3072], P('row', 'col'), may hold values from -0.1875 to 0.1875
- out_weight: bfloat16 [1024, 1024], P('col', 'row'), may hold values from -0.75 to 0.75
- norm_second: bfloat16 [1024], P(('row', 'col')), may hold values from 0.099609375 to 1.8984375
- up_weight: bfloat16 [1024, 4096], P('row', 'col'), may hold values from -0.1875 to 0.1875
- down_weight: bfloat16 [4096, 1024], P('col', 'row'), may hold values from -0.09375 to 0.09375
- route_index: int32 [288, 128], P(('row', 'col')), may hold values from 0 to 1023, as said below
- out_cotangent: bfloat16 [294912, 1024], P(('row', 'col')), may hold values from -6 to 6
Outputs:
- output: bfloat16 [294912, 1024], P(('row', 'col'))
- input_grad: float32 [294912, 1024], P(('row', 'col'))
- router_grad: float32 [1024], P(('row', 'col'))
- norm_first_grad: float32 [1024], P(('row', 'col'))
- qkv_grad: float32 [1024, 3072], P('row', 'col')
- out_grad: float32 [1024, 1024], P('col', 'row')
- norm_second_grad: float32 [1024], P(('row', 'col'))
- up_grad: float32 [1024, 4096], P('row', 'col')
- down_grad: float32 [4096, 1024], P('col', 'row')
The draws below stay inside these ranges and needn't reach their ends.
Inputs may be any that keep to these rules, and one draw needn't show every extreme that they name: `route_index`: each row lists 128 distinct positions of one sequence in increasing order; the first is 0 and the last 1023.
All inputs are finite; a program needn't handle non-finite values.
Results may differ from the reference program's by a relative error of at most 0.019.
Values may be sent and summed in bfloat16 or wider, within the bound.
No kernel may reach another device: no remote copies, remote signals or barrier semaphores. Data moves between devices by JAX's collectives and lax.ppermute only.
A program may use at most 320 MiB of HBM per device.

```python
import jax
import jax.numpy as jnp
from jax import lax

D = 1024
HEADS = 16
HD = 64
FF = 4096
SEQ = 1024
ROUTED = 128
NSEQ = 288
TOKENS = 294912


def draw_route_index(key, part):
    seq_keys = jax.random.split(key, NSEQ)

    def one_sequence(seq_key):
        inner = jax.random.permutation(seq_key, SEQ - 2)[:ROUTED - 2].astype(jnp.int32) + 1
        inner = jnp.sort(inner)
        first = jnp.zeros((1,), jnp.int32)
        last = jnp.full((1,), SEQ - 1, jnp.int32)
        return jnp.concatenate([first, inner, last])
    return jax.vmap(one_sequence)(seq_keys)


def spiked(array, stream_key, source, target, parts, factor):
    def block_of(dim):
        return (jnp.arange(array.shape[dim]) // (array.shape[dim] // parts)).reshape((-1,) + (1,) * (array.ndim - 1 - dim))

    one_side = jax.random.permutation(stream_key, parts)[block_of(target)]
    other_side = (block_of(target) + parts // 2) % parts
    return jnp.where((block_of(source) == one_side) | (block_of(source) == other_side), factor * array, array)


def level_of(stream_key, extent, cuts, low, high):
    def one(dim, parts):
        draws = jax.random.uniform(jax.random.fold_in(jax.random.fold_in(stream_key, 6), dim), (parts,), jnp.float32, low / len(cuts), high / len(cuts))
        return jnp.repeat(jnp.exp(draws), extent[dim] // parts).reshape((-1,) + (1,) * (len(extent) - dim - 1))

    level = one(*cuts[0])
    for cut in cuts[1:]:
        level = level * one(*cut)
    return level


def gaussian(own_key, shape, spread, limit, cuts=(), kind=jnp.bfloat16):
    factor_of = level_of(own_key, shape, cuts, -0.22, 0.18) if cuts else 1.0
    drawn = jax.random.normal(own_key, shape, jnp.float32) * spread * factor_of
    return jnp.minimum(jnp.maximum(drawn, -limit), limit).astype(kind)


def noise_with(rng, extent, spread, reach, cuts, heavy, kind=jnp.bfloat16):
    values = spread * jax.random.normal(rng, extent, jnp.float32)
    if cuts:
        values = values * level_of(rng, extent, cuts, -0.22, 0.18)
    return jnp.clip(spiked(values, jax.random.fold_in(rng, 3), *heavy), -reach, reach).astype(kind)


def setup_inputs(seed: int = 0) -> dict:
    key_list = jax.random.split(jax.random.key(seed), 11)
    tokens = noise_with(key_list[0], (TOKENS, D), 1.0, 6.0, ((0, 32),), (0, 1, 32, 2.75))
    router_weight = gaussian(key_list[1], (D,), D ** -0.5, 0.1875, ((0, 32),))
    norm_first = jnp.clip(1.0 + 0.18 * jax.random.normal(key_list[2], (D,), jnp.float32), 0.099609375, 1.8984375).astype(jnp.bfloat16)
    qkv_weight = gaussian(key_list[3], (D, 3 * D), D ** -0.5, 0.1875, ((0, 4), (1, 8)))
    out_weight = gaussian(key_list[4], (D, D), (D // 16) ** -0.5, 0.75, ((0, 8), (1, 4)))
    norm_second = jnp.clip(1.0 + 0.18 * jax.random.normal(key_list[5], (D,), jnp.float32), 0.099609375, 1.8984375).astype(jnp.bfloat16)
    up_weight = gaussian(key_list[6], (D, FF), D ** -0.5, 0.1875, ((0, 4), (1, 8)))
    down_weight = gaussian(key_list[7], (FF, D), FF ** -0.5, 0.09375, ((0, 8), (1, 4)))
    route_index = draw_route_index(jax.random.fold_in(key_list[10], 71), 0)
    out_cotangent = noise_with(key_list[9], (TOKENS, D), 1.0, 6.0, ((0, 32),), (0, 1, 32, 2.75))
    return {"tokens": tokens, "router_weight": router_weight, "norm_first": norm_first, "qkv_weight": qkv_weight, "out_weight": out_weight, "norm_second": norm_second, "up_weight": up_weight, "down_weight": down_weight, "route_index": route_index, "out_cotangent": out_cotangent}


epsilon = 1e-06

@jax.custom_vjp
def low(v):
    return lax.optimization_barrier(v.astype(jnp.bfloat16)).astype(jnp.float32)

@jax.custom_vjp
def low_back(v):
    return v

def low_keep(v):
    return (low(v), None)

def low_pass(kept, grad):
    return (grad,)

def back_keep(v):
    return (v, None)

def back_low(kept, grad):
    return (low(grad),)
low.defvjp(low_keep, low_pass)
low_back.defvjp(back_keep, back_low)

def normalize(field, gain):
    inverse = lax.rsqrt(lax.optimization_barrier(jnp.mean(field * field, axis=-1, keepdims=True)) + epsilon)
    return field * inverse * gain

def forward(tokens, router_weight, norm_first, qkv_weight, out_weight, norm_second, up_weight, down_weight, token_rows):
    highest = lax.Precision.HIGHEST
    picked = tokens[token_rows]
    gate_value = jax.nn.sigmoid(jnp.dot(picked, router_weight, precision=highest))
    normed = low(normalize(picked, norm_first))
    projected = low_back(low(jnp.dot(normed, qkv_weight, precision=highest)))
    heads_qkv = projected.reshape(NSEQ, ROUTED, HEADS, 3, HD)
    queries = heads_qkv[:, :, :, 0]
    key_rows = heads_qkv[:, :, :, 1]
    values = heads_qkv[:, :, :, 2]
    scores = low_back(jnp.einsum('sqhe,skhe->shqk', queries, key_rows, precision=highest) * HD ** (-0.5))
    places = jnp.arange(ROUTED, dtype=jnp.int32)
    causal = places[:, None] >= places[None, :]
    scores = jnp.where(causal, scores, -1e+30)
    attn_probs = low(jax.nn.softmax(scores, axis=-1))
    mixed = jnp.einsum('shqk,skhe->sqhe', attn_probs, values, precision=highest)
    context = low_back(low(mixed.reshape(NSEQ * ROUTED, D)))
    attn_out = low_back(jnp.dot(context, out_weight, precision=highest))
    middle = picked + attn_out
    normed_mid = low(normalize(middle, norm_second))
    pre_act = low_back(jnp.dot(normed_mid, up_weight, precision=highest))
    hidden = low(jax.nn.gelu(pre_act))
    mlp_out = low_back(jnp.dot(hidden, down_weight, precision=highest))
    return tokens.at[token_rows].add(gate_value[:, None] * (attn_out + mlp_out))

def reference(tokens, router_weight, norm_first, qkv_weight, out_weight, norm_second, up_weight, down_weight, route_index, out_cotangent):
    starts = jnp.arange(NSEQ, dtype=jnp.int32) * SEQ
    token_rows = (route_index.astype(jnp.int32) + starts[:, None]).reshape(-1)
    inputs = (tokens, router_weight, norm_first, qkv_weight, out_weight, norm_second, up_weight, down_weight)
    inputs = tuple((item.astype(jnp.float32) for item in inputs))

    def apply_layer(*params):
        return forward(*params, token_rows)
    result, pullback = jax.vjp(apply_layer, *inputs)
    grads = pullback(out_cotangent.astype(jnp.float32))
    return (result.astype(jnp.bfloat16), grads[0], grads[1], grads[2], grads[3], grads[4], grads[5], grads[6], grads[7])
```

```python
import functools
import math

import jax
import jax.numpy as jnp
from jax import lax
from jax.experimental import pallas as pl
from jax.experimental.pallas import tpu as pltpu
from jax.sharding import PartitionSpec as P

HEADS = 16
HD = 64
EPSILON = 1e-06
F32 = jnp.float32
BF16 = jnp.bfloat16
BOTH = ("row", "col")
SLOW = 1

NN = (((1,), (0,)), ((), ()))
NT = (((1,), (1,)), ((), ()))
TN = (((0,), (0,)), ((), ()))


def mul(a, b, dims=NN):
    return lax.dot_general(a, b, dims, preferred_element_type=F32)


def call(
    body, name, grid, ins, outs, shapes, scratch=(), prefetch=0, flops=0, nbytes=0, deps=(), alias=None
):
    count = prefetch + len(ins)

    def run(*refs):
        body(*refs[:count], *refs[count + len(deps) :])

    made = pl.pallas_call(
        run,
        name=name,
        grid_spec=pltpu.PrefetchScalarGridSpec(
            num_scalar_prefetch=prefetch,
            grid=grid,
            in_specs=ins + [pl.BlockSpec(memory_space=pl.ANY)] * len(deps),
            out_specs=outs,
            scratch_shapes=list(scratch),
        ),
        out_shape=shapes,
        input_output_aliases=alias or {},
        compiler_params=pltpu.CompilerParams(
            dimension_semantics=("arbitrary",) * len(grid),
            vmem_limit_bytes=56 * 1024 * 1024,
        ),
        cost_estimate=pl.CostEstimate(
            flops=flops // SLOW, transcendentals=0, bytes_accessed=nbytes // SLOW
        ),
    )
    return lambda *args: made(*args, *deps)


def tied(value, *deps):
    return call(
        lambda given, out: None,
        "tied",
        (1,),
        [pl.BlockSpec(memory_space=pl.ANY)],
        pl.BlockSpec(memory_space=pl.ANY),
        shaped(value.shape, value.dtype),
        deps=deps,
        alias={0: 0},
    )(value)


def whole(shape):
    return pl.BlockSpec(shape, lambda *_: (0,) * len(shape))


def shaped(shape, dtype):
    return jax.ShapeDtypeStruct(shape, dtype)


def one_hot(index_ref, length):
    places = lax.broadcasted_iota(jnp.int32, (length, index_ref.shape[-1]), 0)
    return places == index_ref[0]


def pick_body(index, tok, cot, gain, router, picked, grows, normed, gmlp, gate, base):
    hot = jnp.where(one_hot(index, tok.shape[0]), 1.0, 0.0).astype(BF16)
    rows = mul(hot, tok[...], TN)
    back = mul(hot, cot[...], TN)
    opened = jax.nn.sigmoid(jnp.sum(rows * router[...], axis=-1, keepdims=True))
    inverse = lax.rsqrt(jnp.mean(rows * rows, axis=-1, keepdims=True) + EPSILON)
    picked[...] = rows.astype(BF16)
    grows[...] = back.astype(BF16)
    normed[...] = (rows * inverse * gain[...]).astype(BF16)
    gmlp[...] = (back * opened).astype(BF16)
    gate[...] = opened
    base[...] = cot[...].astype(F32)


def pick(tokens, cotangent, index, gain, router, deps=()):
    seqs, _, routed = index.shape
    length, width = tokens.shape[0] // seqs, tokens.shape[1]
    rows = seqs * routed
    whole_seq = pl.BlockSpec((length, width), lambda s: (s, 0))
    part = pl.BlockSpec((routed, width), lambda s: (s, 0))
    return call(
        pick_body,
        "pick",
        (seqs,),
        [pl.BlockSpec((1, 1, routed), lambda s: (s, 0, 0)), whole_seq, whole_seq]
        + [whole((1, width))] * 2,
        [part] * 4 + [pl.BlockSpec((routed, 1), lambda s: (s, 0)), whole_seq],
        [shaped((rows, width), BF16)] * 4 + [shaped((rows, 1), F32), shaped(tokens.shape, F32)],
        flops=4 * rows * length * width,
        nbytes=4 * tokens.size + 8 * rows * width,
        deps=deps,
    )(index, tokens, cotangent, gain, router)


def lay_rc(w, buf, kb):
    rs, cs, tall, wp = w.shape
    pieces = tall // kb
    for r in range(rs):
        for c in range(cs):
            for t in range(pieces):
                at = (c * pieces + t) * wp
                buf[r * kb : (r + 1) * kb, at : at + wp] = w[r, c, t * kb : (t + 1) * kb, :]


def lay_cr(w, buf, kb):
    rs, cs, tall, wp = w.shape
    pieces = tall // kb
    for r in range(rs):
        for c in range(cs):
            for t in range(pieces):
                at = (r * pieces + t) * wp
                buf[c * kb : (c + 1) * kb, at : at + wp] = w[r, c, t * kb : (t + 1) * kb, :]


def lay_turned(spots, own, other, place, rs, zs):
    bit = spots[2, 0]
    for core in range(2):

        @pl.when(bit == core)
        def _():
            for r in range(rs):
                for z in range(zs):
                    place(r, z, core, own)
                    place(r, z, 1 - core, other)


def project_body(kb, wp, count, spots, x, own_a, own_b, other_a, other_b, out, natural):
    rs = own_a.shape[0]
    tall = own_a.shape[2]

    def place(r, z, core, halves_of):
        size = kb // 2
        for t in range(2 * count):
            half, at = divmod(t * size, tall)
            value = halves_of[half][spots[half, r], 0, at : at + size, :]
            lane = (core * count + t // 2) * wp
            down = r * kb + t % 2 * size
            natural[down : down + size, lane : lane + wp] = value

    lay_turned(spots, (own_a, own_b), (other_a, other_b), place, rs, 1)
    out[...] = mul(x[...], natural[...]).astype(BF16)


def project(spots, x, parts, kb, count):
    rows, depth = x.shape
    rs, zs, tall, wp = parts[0].shape
    step = 2 * count * wp
    piece = pl.BlockSpec((rs, 1, tall, wp), lambda j, spots: (0, spots[3, j], 0, 0))
    return call(
        functools.partial(project_body, kb, wp, count),
        "project",
        (zs,),
        [pl.BlockSpec(x.shape, lambda j, _: (0, 0))] + [piece] * 4,
        [
            pl.BlockSpec((rows, step), lambda j, _: (0, j)),
            pl.BlockSpec((depth, step), lambda j, _: (0, j)),
        ],
        [shaped((rows, zs * step), BF16), shaped((depth, zs * step), BF16)],
        prefetch=1,
        flops=2 * rows * depth * zs * step,
        nbytes=2 * (x.size + 2 * depth * zs * step + rows * zs * step),
    )(spots, x, *parts)


def halves():
    lane = lax.broadcasted_iota(jnp.int32, (1, 2 * HD), 1)
    low = jnp.where(lane < HD, 1.0, 0.0).astype(BF16)
    high = jnp.where(lane < HD, 0.0, 1.0).astype(BF16)
    return low, high


def turned(x):
    return jnp.concatenate([x[:, HD:], x[:, :HD]], axis=1) * jnp.asarray(HD**-0.5, BF16)


def softmax(scores, causal):
    scores = jnp.where(causal, scores, -1e30)
    expanded = jnp.exp(scores - jnp.max(scores, axis=0, keepdims=True))
    return (expanded * (1.0 / jnp.sum(expanded, axis=0, keepdims=True))).astype(BF16)


def causal_of(routed):
    return lax.broadcasted_iota(jnp.int32, (routed, routed), 0) <= lax.broadcasted_iota(
        jnp.int32, (routed, routed), 1
    )


def attend_body(proj, context, probs):
    routed = proj.shape[0]
    low, high = halves()
    causal = causal_of(routed)
    for pair in range(HEADS // 2):
        a, b, c = (proj[:, (3 * pair + t) * 2 * HD : (3 * pair + t + 1) * 2 * HD] for t in range(3))
        first = softmax(mul(turned(a) * low, a, NT), causal)
        second = softmax(mul(turned(c) * high, b, NT), causal)
        both = jnp.concatenate([first, second], axis=0)
        probs[0, 2 * pair * routed : 2 * (pair + 1) * routed, :] = both
        mixed = mul(both, jnp.concatenate([b * low, c * high], axis=0), TN)
        context[:, pair * 2 * HD : (pair + 1) * 2 * HD] = mixed.astype(BF16)


def attend(projected, seqs):
    rows, wide = projected.shape
    routed = rows // seqs
    width = wide // 3
    return call(
        attend_body,
        "attend",
        (seqs,),
        [pl.BlockSpec((routed, wide), lambda s: (s, 0))],
        [
            pl.BlockSpec((routed, width), lambda s: (s, 0)),
            pl.BlockSpec((1, HEADS * routed, routed), lambda s: (s, 0, 0)),
        ],
        [shaped((rows, width), BF16), shaped((seqs, HEADS * routed, routed), BF16)],
        flops=20 * rows * wide * routed,
        nbytes=8 * projected.size,
    )(projected)


def mix_body(kb, context, w, picked, gain, attn, normed, natural):
    @pl.when(pl.program_id(0) == 0)
    def _():
        lay_cr(w, natural, kb)

    out = mul(context[...], natural[...])
    attn[...] = out
    middle = picked[...].astype(F32) + out
    inverse = lax.rsqrt(jnp.mean(middle * middle, axis=-1, keepdims=True) + EPSILON)
    normed[...] = (middle * inverse * gain[...]).astype(BF16)


def mix(context, w, at, tall, kb, picked, gain, steps):
    rows, width = context.shape
    rs, cs, _, wp = w.shape
    part = pl.BlockSpec((rows // steps, width), lambda s: (s, 0))
    return call(
        functools.partial(mix_body, kb),
        "mix",
        (steps,),
        [part, pl.BlockSpec((rs, cs, tall, wp), lambda s: (0, 0, at, 0)), part, whole(gain.shape)],
        [part, part, whole((width, width))],
        [shaped((rows, width), F32), shaped((rows, width), BF16), shaped((width, width), BF16)],
        flops=2 * rows * width * width,
        nbytes=14 * rows * width,
    )(context, w, picked, gain)


GELU_A = 0.7978845608028654
GELU_B = 0.044715


def raise_body(kb, x, w, hidden, slope, natural):
    lay_rc(w, natural, kb)
    rows, step = hidden.shape
    tall, tile = rows // 3, 256
    for n in range(step // tile):
        across = slice(n * tile, (n + 1) * tile)
        for m in range(rows // tall):
            down = slice(m * tall, (m + 1) * tall)
            pre = mul(x[down, :], natural[:, across])
            square = pre * pre
            bent = jnp.tanh(pre * (GELU_A + (GELU_A * GELU_B) * square))
            half = 0.5 + 0.5 * bent
            hidden[down, across] = (pre * half).astype(BF16)
            slope[down, across] = (
                half
                + (0.5 * pre)
                * (1.0 - bent * bent)
                * (GELU_A + (3 * GELU_A * GELU_B) * square)
            ).astype(BF16)


def raised(x, w, at, tall, kb, count):
    rows, depth = x.shape
    rs, cs, _, wp = w.shape
    wide = cs * (tall // kb) * wp
    many = cs // count
    step = wide // count
    out = pl.BlockSpec((rows, step), lambda j: (0, j))
    return call(
        functools.partial(raise_body, kb),
        "raise",
        (count,),
        [whole(x.shape), pl.BlockSpec((rs, many, tall, wp), lambda j: (0, j, at, 0))],
        [out, out, pl.BlockSpec((depth, step), lambda j: (0, j))],
        [shaped((rows, wide), BF16)] * 2 + [shaped((depth, wide), BF16)],
        flops=3 * rows * depth * wide,
        nbytes=2 * (x.size + 2 * depth * wide + 2 * rows * wide),
    )(x, w)


def split_out(bit, first, second, keep, send, at):
    @pl.when(bit == 0)
    def _():
        keep[at] = first
        send[at] = second

    @pl.when(bit != 0)
    def _():
        keep[at] = second
        send[at] = first


def grad_rc(bit, total, send, keep, kb, nb):
    rs, zs, _, wp = send.shape
    for r in range(rs):
        for j in range(zs):
            for t in range(nb // wp):
                at = 2 * j * nb + t * wp
                down = slice(r * kb, (r + 1) * kb)
                where = (r, j, slice(t * kb, (t + 1) * kb))
                split_out(
                    bit, total[down, at : at + wp], total[down, at + nb : at + nb + wp], keep, send, where
                )


def grad_rc_body(kb, nb, bit, x, y, send, keep):
    grad_rc(bit[0], mul(x[...], y[...], TN).astype(BF16), send, keep, kb, nb)


def grad_cr(bit, total, send, keep, kb, nb):
    rs, zs, _, wp = send.shape
    for r in range(rs):
        for j in range(zs):
            for t in range(nb // wp):
                across = slice(r * nb + t * wp, r * nb + (t + 1) * wp)
                where = (r, j, slice(t * kb, (t + 1) * kb))
                at = 2 * j * kb
                split_out(
                    bit, total[at : at + kb, across], total[at + kb : at + 2 * kb, across], keep, send, where
                )


def grad_cr_body(kb, nb, bit, x, y, send, keep):
    grad_cr(bit[0], mul(x[...], y[...], TN).astype(BF16), send, keep, kb, nb)


def weight_grad(name, bit, x, y, shape, wp, by_row, count, deps=()):
    rows = x.shape[0]
    rs, cs, kb, nb = shape
    zs = cs // 2
    many = zs // count
    tall = kb * nb // wp
    cut = pl.BlockSpec((rows, 2 * many * (nb if by_row else kb)), lambda j, _: (0, j))
    out = pl.BlockSpec((rs, many, tall, wp), lambda j, _: (0, j, 0, 0))
    return call(
        functools.partial(grad_rc_body if by_row else grad_cr_body, kb, nb),
        name,
        (count,),
        [whole(x.shape), cut] if by_row else [cut, whole(y.shape)],
        [out, out],
        [shaped((rs, zs, tall, wp), BF16)] * 2,
        prefetch=1,
        flops=2 * rows * rs * cs * kb * nb,
        nbytes=2 * (x.size + y.size + rs * cs * kb * nb),
        deps=deps,
    )(bit, x, y)


def qkv_grad_body(kb, nb, bit, x, y, w, send, keep, first):
    total = mul(x[...], y[...], TN)

    @pl.when(pl.program_id(0) == 0)
    def _():
        first[...] = jnp.zeros_like(first)

    first[...] += jnp.sum(total * w[...].astype(F32), axis=-1, keepdims=True)
    grad_rc(bit[0], total.astype(BF16), send, keep, kb, nb)


def qkv_weight_grad(bit, x, y, w, shape, wp, count):
    rows, depth = x.shape
    rs, cs, kb, nb = shape
    zs = cs // 2
    many = zs // count
    tall = kb * nb // wp
    step = 2 * many * nb
    out = pl.BlockSpec((rs, many, tall, wp), lambda j, _: (0, j, 0, 0))
    return call(
        functools.partial(qkv_grad_body, kb, nb),
        "qkv_grad",
        (count,),
        [
            whole(x.shape),
            pl.BlockSpec((rows, step), lambda j, _: (0, j)),
            pl.BlockSpec((depth, step), lambda j, _: (0, j)),
        ],
        [out, out, whole((depth, 1))],
        [shaped((rs, zs, tall, wp), BF16)] * 2 + [shaped((depth, 1), F32)],
        prefetch=1,
        flops=2 * rows * depth * cs * nb,
        nbytes=2 * (x.size + y.size + 2 * w.size),
    )(bit, x, y, w)


def lower_body(hidden, w, attn, picked, gate, kept):
    branch = attn[...] + mul(hidden[...], w[...])
    kept[...] = (picked[...].astype(F32) + gate[...] * branch).astype(BF16)


def lowered(hidden, w, attn, picked, gate, step, deps=()):
    rows, deep = hidden.shape
    width = w.shape[1]
    cut = pl.BlockSpec((rows, step), lambda j: (0, j))
    return call(
        lower_body,
        "lower",
        (width // step,),
        [whole(hidden.shape), pl.BlockSpec((deep, step), lambda j: (0, j))]
        + [cut] * 2
        + [whole(gate.shape)],
        cut,
        shaped((rows, width), BF16),
        flops=2 * rows * deep * width,
        nbytes=2 * (hidden.size + w.size) + 8 * attn.size,
        deps=deps,
    )(hidden, w, attn, picked, gate)


def hidden_back_body(kb, grows, w, slope, hidden, gate, out, natural, dots):
    lay_cr(w, natural, kb)
    tile = 128

    @pl.when(pl.program_id(0) == 0)
    def _():
        dots[...] = jnp.zeros_like(dots)

    back = mul(grows[...], natural[...], NT)
    out[...] = (back * gate[...] * slope[...].astype(F32)).astype(BF16)
    product = back * hidden[...].astype(F32)
    summed = product[:, :tile]
    for n in range(1, product.shape[1] // tile):
        summed = summed + product[:, n * tile : (n + 1) * tile]
    dots[...] += summed


def hidden_back(grows, w, tall, kb, slope, hidden, gate, count, deps=()):
    rows, width = grows.shape
    rs, cs, _, wp = w.shape
    many = cs // count
    step = many * kb
    cut = pl.BlockSpec((rows, step), lambda j: (0, j))
    return call(
        functools.partial(hidden_back_body, kb),
        "hidden_back",
        (count,),
        [whole(grows.shape), pl.BlockSpec((rs, many, tall, wp), lambda j: (0, j, 0, 0)), cut, cut]
        + [whole(gate.shape)],
        [cut, pl.BlockSpec((step, width), lambda j: (j, 0)), whole((rows, 128))],
        [
            shaped((rows, cs * kb), BF16),
            shaped((cs * kb, width), BF16),
            shaped((rows, 128), F32),
        ],
        flops=2 * rows * width * cs * kb,
        nbytes=2 * (grows.size + 2 * cs * kb * width + 3 * slope.size),
        deps=deps,
    )(grows, w, slope, hidden, gate)


def norm_back(grad, v, inverse, gain):
    scaled = grad * gain
    summed = jnp.sum(scaled * v, axis=-1, keepdims=True)
    return inverse * scaled - v * (inverse * inverse * inverse * summed / v.shape[-1])


def middle_back_body(
    gpre, w, attn, picked, grows, gate, gain, dots, gmid, gattn, gsmall, logit, total
):
    j = pl.program_id(0)
    step = w.shape[0]
    for i in range(total.shape[1] // step):

        @pl.when(j == i)
        def _():
            total[:, i * step : (i + 1) * step] = mul(gpre[...], w[...], NT)

    @pl.when(j == pl.num_programs(0) - 1)
    def _():
        summed = jnp.zeros_like(gain)
        routing = jnp.zeros_like(gain)
        chunk = 128
        for i in range(total.shape[0] // chunk):
            at = slice(i * chunk, (i + 1) * chunk)
            grad = total[at, :]
            rows = picked[at, :].astype(F32)
            middle = rows + attn[at, :]
            inverse = lax.rsqrt(jnp.mean(middle * middle, axis=-1, keepdims=True) + EPSILON)
            summed += jnp.sum(grad * middle * inverse, axis=0, keepdims=True)
            back = norm_back(grad, middle, inverse, gain[...])
            gmid[at, :] = back
            opened, dy = gate[at, :], grows[at, :].astype(F32)
            gattn[at, :] = (opened * dy + back).astype(BF16)
            opening = jnp.sum(dots[at, :], axis=-1, keepdims=True)
            opening += jnp.sum(dy * attn[at, :], axis=-1, keepdims=True)
            opening = opening * opened * (1.0 - opened)
            logit[at, :] = opening
            routing += jnp.sum(opening * rows, axis=0, keepdims=True)
        gsmall[0:1, :] = summed
        gsmall[1:2, :] = routing


def middle_back(gpre, w, attn, picked, grows, gate, gain, dots, step, deps=()):
    rows, deep = gpre.shape
    width = attn.shape[1]
    return call(
        middle_back_body,
        "middle_back",
        (width // step,),
        [whole(gpre.shape), pl.BlockSpec((step, deep), lambda j: (j, 0))]
        + [whole(t.shape) for t in (attn, picked, grows, gate, gain, dots)],
        [whole(attn.shape), whole(attn.shape), whole((2, width)), whole(gate.shape)],
        [
            shaped(attn.shape, F32),
            shaped(attn.shape, BF16),
            shaped((2, width), F32),
            shaped(gate.shape, F32),
        ],
        [pltpu.VMEM((rows, width), F32)],
        flops=2 * rows * deep * width,
        nbytes=2 * (gpre.size + w.size) + 14 * attn.size,
        deps=deps,
    )(gpre, w, attn, picked, grows, gate, gain, dots)


def context_back_body(kb, nb, bit, gattn, w, context, gcontext, send, keep):
    gcontext[...] = mul(gattn[...], w[...], NT).astype(BF16)
    grad_cr_body(kb, nb, bit, context, gattn, send, keep)


def context_back(bit, gattn, w, context, shape, wp):
    rows, width = gattn.shape
    rs, cs, kb, nb = shape
    half = (rs, cs // 2, kb * nb // wp, wp)
    return call(
        functools.partial(context_back_body, kb, nb),
        "context_back",
        (1,),
        [whole(gattn.shape), whole(w.shape), whole(context.shape)],
        [whole(context.shape), whole(half), whole(half)],
        [shaped(context.shape, BF16), shaped(half, BF16), shaped(half, BF16)],
        prefetch=1,
        flops=4 * rows * width * width,
        nbytes=6 * rows * width + 4 * width * width,
    )(bit, gattn, w, context)


def attend_back_body(proj, gcontext, probs, out):
    routed = proj.shape[0]
    low, high = halves()

    def scores_back(grad_probs, weights):
        weights = weights.astype(F32)
        inner = jnp.sum(grad_probs * weights, axis=0, keepdims=True)
        return (weights * (grad_probs - inner)).astype(BF16)

    for pair in range(HEADS // 2):
        at = [slice((3 * pair + t) * 2 * HD, (3 * pair + t + 1) * 2 * HD) for t in range(3)]
        a, b, c = (proj[:, cut] for cut in at)
        grad = gcontext[:, pair * 2 * HD : (pair + 1) * 2 * HD]
        grad_low, grad_high = grad * low, grad * high
        a_turned, b_turned, c_turned = turned(a), turned(b), turned(c)
        first = probs[0, 2 * pair * routed : (2 * pair + 1) * routed, :]
        second = probs[0, (2 * pair + 1) * routed : 2 * (pair + 1) * routed, :]
        back_first = scores_back(mul(b, grad_low, NT), first)
        back_second = scores_back(mul(c, grad_high, NT), second)
        out[:, at[0]] = (
            mul(back_first, a_turned * low, TN) + mul(back_first, a_turned * high)
        ).astype(BF16)
        out[:, at[1]] = (
            mul(first, grad_low) + mul(back_second, c_turned * high, TN)
        ).astype(BF16)
        out[:, at[2]] = (mul(back_second, b_turned * low) + mul(second, grad_high)).astype(BF16)


def attend_back(projected, gcontext, probs, seqs, deps=()):
    rows, wide = projected.shape
    routed = rows // seqs
    return call(
        attend_back_body,
        "attend_back",
        (seqs,),
        [
            pl.BlockSpec((routed, wide), lambda s: (s, 0)),
            pl.BlockSpec((routed, wide // 3), lambda s: (s, 0)),
            pl.BlockSpec((1, HEADS * routed, routed), lambda s: (s, 0, 0)),
        ],
        pl.BlockSpec((routed, wide), lambda s: (s, 0)),
        shaped((rows, wide), BF16),
        flops=40 * rows * wide * routed,
        nbytes=16 * projected.size,
        deps=deps,
    )(projected, gcontext, probs)


def picked_back_body(
    places, gproj, w, picked, gmid, logit, grows, gain, router, base, out, total, arrived
):
    j = pl.program_id(0)
    step = w.shape[0]
    for i in range(total.shape[1] // step):

        @pl.when(j == i)
        def _():
            total[:, i * step : (i + 1) * step] = mul(gproj[...], w[...], NT)

    @pl.when(j == pl.num_programs(0) - 1)
    def _():
        chunk = 128
        for i in range(total.shape[0] // chunk):
            at = slice(i * chunk, (i + 1) * chunk)
            grad = total[at, :]
            rows = picked[at, :].astype(F32)
            inverse = lax.rsqrt(jnp.mean(rows * rows, axis=-1, keepdims=True) + EPSILON)
            back = norm_back(grad, rows, inverse, gain[...])
            total[at, :] = (
                gmid[at, :] + back + (logit[at, :] * router[...] + grows[at, :].astype(F32))
            )

            def send(k, carry):
                pltpu.make_async_copy(
                    total.at[pl.ds(k, 1)], out.at[pl.ds(places[k], 1)], arrived
                ).start()
                return carry

            lax.fori_loop(i * chunk, (i + 1) * chunk, send, 0, unroll=8)
        pltpu.make_async_copy(total, out.at[pl.ds(0, total.shape[0])], arrived).wait()


def picked_back(places, gproj, w, picked, gmid, logit, grows, gain, router, base, step, deps=()):
    rows, deep = gproj.shape
    width = picked.shape[1]
    return call(
        picked_back_body,
        "picked_back",
        (width // step,),
        [whole(gproj.shape), pl.BlockSpec((step, deep), lambda j, _: (j, 0))]
        + [whole(t.shape) for t in (picked, gmid, logit, grows, gain, router)]
        + [pl.BlockSpec(memory_space=pl.ANY)],
        pl.BlockSpec(memory_space=pl.ANY),
        shaped(base.shape, F32),
        [pltpu.VMEM((rows, width), F32), pltpu.SemaphoreType.DMA],
        prefetch=1,
        flops=2 * rows * deep * width,
        nbytes=2 * (gproj.size + w.size) + 10 * picked.size,
        alias={9: 0},
        deps=deps,
    )(places, gproj, w, picked, gmid, logit, grows, gain, router, base)


def join_body(count, *refs):
    out, at = refs[-1], 0
    for keep, got in zip(refs[:count], refs[count : 2 * count]):
        tall = keep.shape[2]
        out[:, :, at : at + tall] = (keep[...].astype(F32) + got[...].astype(F32)).astype(BF16)
        at += tall


def joined(keeps, gots, deps=()):
    rs, zs, _, wp = keeps[0].shape
    talls = [k.shape[2] for k in keeps]
    blocks = [pl.BlockSpec((1, zs, tall, wp), lambda r: (r, 0, 0, 0)) for tall in talls]
    tall = sum(talls)
    return call(
        functools.partial(join_body, len(keeps)),
        "join",
        (rs,),
        blocks * 2,
        pl.BlockSpec((1, zs, tall, wp), lambda r: (r, 0, 0, 0)),
        shaped((rs, zs, tall, wp), BF16),
        flops=rs * zs * tall * wp,
        nbytes=6 * rs * zs * tall * wp,
        deps=deps,
    )(*keeps, *gots)


def place_body(index, tok, kept, output):
    found = one_hot(index, tok.shape[0])
    hot = jnp.where(found, 1.0, 0.0)
    routed = jnp.sum(hot, axis=-1, keepdims=True) > 0.5
    output[...] = jnp.where(
        routed, mul(hot.astype(BF16), kept[...]), tok[...].astype(F32)
    ).astype(BF16)


def place(tokens, index, kept, deps=()):
    seqs, _, routed = index.shape
    length, width = tokens.shape[0] // seqs, tokens.shape[1]
    whole_seq = pl.BlockSpec((length, width), lambda s: (s, 0))
    return call(
        place_body,
        "place",
        (seqs,),
        [
            pl.BlockSpec((1, 1, routed), lambda s: (s, 0, 0)),
            whole_seq,
            pl.BlockSpec((routed, width), lambda s: (s, 0)),
        ],
        whole_seq,
        shaped(tokens.shape, BF16),
        flops=2 * seqs * routed * length * width,
        nbytes=4 * tokens.size,
        deps=deps,
    )(index, tokens, kept)


def pieces(block, wp):
    return [block[:, i : i + wp] for i in range(0, block.shape[1], wp)]


def gathered(flat, rs, cs):
    return lax.all_gather(flat, BOTH, axis=0, tiled=True).reshape(rs, cs, *flat.shape)


def shifted(value, part, shift, rs, cs):
    side = math.isqrt(rs)
    if part == "x":
        moves = [(r, r // side * side + (r + shift) % side) for r in range(rs)]
    elif part == "y":
        moves = [(r, (r + shift * side) % rs) for r in range(rs)]
    else:
        moves = [(c, (c + 2 * shift) % cs) for c in range(cs)]
    return lax.ppermute(value, "col" if part == "z" else "row", moves)


def permuted(flat, rs, cs, early, beside):
    side, zs = math.isqrt(rs), cs // 2
    line = [flat] + [shifted(flat, "z", i, rs, cs) for i in range(1, zs)]
    tall = flat.shape[0] // 2
    held = [jnp.stack([part[h * tall : (h + 1) * tall] for part in line])[None] for h in range(2)]
    held[0] = tied(held[0], early)
    held = [
        jnp.concatenate([h] + [shifted(h, part, i, rs, cs) for i in range(1, side)])
        for h, part in zip(held, "xy")
    ]
    moved = [
        [shifted(h, part, i, rs, cs) for i in range(1, side)] for h, part in zip(held, "yx")
    ]
    extra = beside(held[1])
    held = [jnp.concatenate([tied(h, extra[0])] + m) for h, m in zip(held, moved)]
    pairs = [(c, c ^ 1) for c in range(cs)]
    return held + [lax.ppermute(h, "col", pairs) for h in held], extra


def spots_of(rs, cs):
    side, zs = math.isqrt(rs), cs // 2
    row, column = lax.axis_index("row"), lax.axis_index("col")
    r, z = jnp.arange(rs), jnp.arange(zs)
    y, x = (row // side - r // side) % side, (row - r) % side
    table = jnp.zeros((4, max(rs, zs)), jnp.int32)
    table = table.at[0, :rs].set(y * side + x).at[1, :rs].set(x * side + y)
    return table.at[2, :].set(column % 2).at[3, :zs].set((column // 2 - z) % zs)


def after(value, *others):
    return lax.optimization_barrier((value, *others))[0]


def local(
    tokens,
    router_weight,
    norm_first,
    qkv_weight,
    out_weight,
    norm_second,
    up_weight,
    down_weight,
    route_index,
    out_cotangent,
    rs,
    cs,
):
    seqs, routed = route_index.shape
    width = tokens.shape[1]
    index = route_index.reshape(seqs, 1, routed)
    column = lax.axis_index("col")
    core, depth = column % 2, column // 2
    zs = cs // 2
    bit = core.astype(jnp.int32).reshape(1)
    pairs = [(c, c ^ 1) for c in range(cs)]
    blocks = [w.shape for w in (qkv_weight, out_weight, up_weight, down_weight)]
    shape_qkv, shape_out, shape_up, shape_down = ((rs, cs) + b for b in blocks)
    wp = math.gcd(128, *(b[1] for b in blocks))
    tall_qkv, tall_out, tall_up, tall_down = (b[0] * b[1] // wp for b in blocks)

    spots = spots_of(rs, cs)
    small = jnp.stack([router_weight, norm_first, norm_second])
    small = lax.all_gather(lax.all_gather(small, "col", axis=0), "row", axis=0)
    small = small.reshape(rs * cs, 3, -1).transpose(1, 0, 2).reshape(3, 1, width).astype(F32)
    router, first_gain, second_gain = small[0], small[1], small[2]
    parts, (picked, grows, normed, gmlp, gate, base) = permuted(
        jnp.concatenate(pieces(qkv_weight, wp)),
        rs,
        cs,
        small,
        lambda dep: pick(tokens, out_cotangent, index, first_gain, router, deps=(dep,)),
    )
    next_parts = gathered(jnp.concatenate(pieces(up_weight, wp) + pieces(out_weight, wp)), rs, cs)
    down_parts = gathered(jnp.concatenate(pieces(down_weight, wp)), rs, cs)

    def exchanged(send):
        return lax.ppermute(send, "col", pairs)

    def by_row(keep):
        r, z, tall, _ = keep.shape
        mine = lax.psum_scatter(
            keep.reshape(r * z * tall, wp), "row", scatter_dimension=0, tiled=True
        )
        return mine.reshape(z, tall, wp)

    def by_depth(mine):
        total = lax.dynamic_index_in_dim(mine, depth, 0, keepdims=False).astype(F32)
        for shift in range(1, zs):
            part = lax.dynamic_index_in_dim(mine, (depth + shift) % zs, 0, keepdims=False)
            total = total + shifted(part, "z", shift, rs, cs).astype(F32)
        return total

    def block(total, shape):
        kb, nb = shape[2:]
        return jnp.concatenate([total[i : i + kb] for i in range(0, kb * nb // wp, kb)], axis=1)

    projected, w_qkv = project(spots, normed, parts, blocks[0][0], blocks[0][1] // wp)
    context, probs = attend(projected, seqs)
    attn, normed_mid, w_out = mix(
        context, next_parts, tall_up // tall_out, tall_out, blocks[1][0], picked, second_gain, 3
    )
    hidden, slope, w_up = raised(normed_mid, next_parts, 0, tall_up, blocks[2][0], 4)

    down_send, down_keep = weight_grad("down_grad", bit, hidden, gmlp, shape_down, wp, False, 4)
    gpre, w_down, dots = hidden_back(
        grows, down_parts, tall_down, blocks[3][0], slope, hidden, gate, 4, deps=(down_send,)
    )
    down_keep = joined([down_keep], [exchanged(down_send)], deps=(gpre,))
    down_rows = by_row(down_keep)

    up_send, up_keep = weight_grad(
        "up_grad", bit, normed_mid, gpre, shape_up, wp, True, 4, deps=(down_keep,)
    )
    gmid, gattn, gsmall, logit = middle_back(
        gpre, w_up, attn, picked, grows, gate, second_gain, dots, 256, deps=(up_send,)
    )
    up_keep = joined([up_keep], [exchanged(up_send)], deps=(gattn,))
    up_rows = by_row(up_keep)
    gattn = tied(gattn, up_keep)
    gcontext, out_send, out_keep = context_back(bit, gattn, w_out, context, shape_out, wp)

    gproj = attend_back(projected, gcontext, probs, seqs, deps=(up_keep,))
    qkv_send, qkv_keep, gfirst = qkv_weight_grad(bit, normed, gproj, w_qkv, shape_qkv, wp, 4)
    little = jnp.concatenate([gsmall, (gfirst / first_gain.reshape(width, 1)).reshape(1, width)])
    little = little.reshape(3, rs, zs, 2, -1).transpose(1, 2, 3, 0, 4)
    little = little.reshape(rs, zs, 2, -1).astype(BF16)
    lines = -(-little.shape[-1] // wp)
    little = jnp.pad(little, ((0, 0),) * 3 + ((0, lines * wp - little.shape[-1]),))
    little = jnp.pad(little.reshape(rs, zs, 2, lines, wp), ((0, 0),) * 3 + ((0, 16 - lines), (0, 0)))
    little_keep = lax.dynamic_index_in_dim(little, core, 2, keepdims=False)
    little_send = lax.dynamic_index_in_dim(little, 1 - core, 2, keepdims=False)
    qkv_keep = joined(
        [qkv_keep, out_keep, little_keep],
        [exchanged(qkv_send), exchanged(out_send), exchanged(little_send)],
    )
    qkv_rows = by_row(qkv_keep)

    kept = lowered(hidden, w_down, attn, picked, gate, 256, deps=(qkv_keep, down_rows))
    down_grad = block(by_depth(down_rows), shape_down)
    starts = jnp.arange(seqs, dtype=jnp.int32) * (tokens.shape[0] // seqs)
    places = (route_index + starts[:, None]).reshape(-1)
    input_grad = picked_back(
        places, gproj, w_qkv, picked, gmid, logit, grows, first_gain, router, base, 256,
        deps=(kept, up_rows),
    )
    up_total = by_depth(up_rows)
    output = place(tokens, index, kept, deps=(input_grad, up_total))
    qkv_total = by_depth(qkv_rows)
    up_grad = block(up_total, shape_up)
    out_grad = block(qkv_total[tall_qkv : tall_qkv + tall_out], shape_out)
    qkv_grad = block(qkv_total[:tall_qkv], shape_qkv)
    lowest = tall_qkv + tall_out
    sums = qkv_total[lowest : lowest + lines].reshape(-1)[: 3 * width // (rs * cs)].reshape(3, -1)
    return (
        output,
        input_grad,
        sums[1],
        sums[2],
        qkv_grad,
        out_grad,
        sums[0],
        up_grad,
        down_grad,
    )


def solution(mesh):
    both, by_row, by_col = P(BOTH), P("row", "col"), P("col", "row")
    tall = P(BOTH, None)
    return jax.shard_map(
        functools.partial(local, rs=mesh.shape["row"], cs=mesh.shape["col"]),
        mesh=mesh,
        in_specs=(tall, both, both, by_row, by_col, both, by_row, by_col, tall, tall),
        out_specs=(tall, tall, both, both, by_row, by_col, both, by_row, by_col),
        check_vma=False,
    )
```

```python
import functools
import math

import jax
import jax.numpy as jnp
from jax import lax
from jax.experimental import pallas as pl
from jax.experimental.pallas import tpu as pltpu
from jax.sharding import PartitionSpec as P

HEADS = 16
HD = 64
EPSILON = 1e-06
F32 = jnp.float32
BF16 = jnp.bfloat16
BOTH = ("row", "col")
SLOW = 1

NN = (((1,), (0,)), ((), ()))
NT = (((1,), (1,)), ((), ()))
TN = (((0,), (0,)), ((), ()))


def mul(a, b, dims=NN):
    return lax.dot_general(a, b, dims, preferred_element_type=F32)


def call(
    body, name, grid, ins, outs, shapes, scratch=(), prefetch=0, flops=0, nbytes=0, deps=(), alias=None, vmem=56
):
    count = prefetch + len(ins)

    def run(*refs):
        body(*refs[:count], *refs[count + len(deps) :])

    made = pl.pallas_call(
        run,
        name=name,
        grid_spec=pltpu.PrefetchScalarGridSpec(
            num_scalar_prefetch=prefetch,
            grid=grid,
            in_specs=ins + [pl.BlockSpec(memory_space=pl.ANY)] * len(deps),
            out_specs=outs,
            scratch_shapes=list(scratch),
        ),
        out_shape=shapes,
        input_output_aliases=alias or {},
        compiler_params=pltpu.CompilerParams(
            dimension_semantics=("arbitrary",) * len(grid),
            vmem_limit_bytes=vmem * 2**20,
        ),
        cost_estimate=pl.CostEstimate(
            flops=flops // SLOW, transcendentals=0, bytes_accessed=nbytes // SLOW
        ),
    )
    return lambda *args: made(*args, *deps)


def tied(value, *deps):
    return call(
        lambda given, out: None,
        "tied",
        (1,),
        [pl.BlockSpec(memory_space=pl.ANY)],
        pl.BlockSpec(memory_space=pl.ANY),
        shaped(value.shape, value.dtype),
        deps=deps,
        alias={0: 0},
        vmem=60,
    )(value)


def whole(shape):
    return pl.BlockSpec(shape, lambda *_: (0,) * len(shape))


def once(shape):
    return pl.BlockSpec(shape, lambda *_: (0,) * len(shape), pipeline_mode=pl.Buffered(1))


def shaped(shape, dtype):
    return jax.ShapeDtypeStruct(shape, dtype)


def one_hot(index_ref, length):
    places = lax.broadcasted_iota(jnp.int32, (length, index_ref.shape[-1]), 0)
    return places == index_ref[0]


def pick_cot_body(index, cot, grows, base):
    hot = jnp.where(one_hot(index, cot.shape[0]), 1.0, 0.0).astype(BF16)
    grows[...] = mul(hot, cot[...], TN).astype(BF16)
    base[...] = cot[...].astype(F32)


def pick_body(index, tok, picked):
    hot = jnp.where(one_hot(index, tok.shape[0]), 1.0, 0.0).astype(BF16)
    picked[...] = mul(hot, tok[...], TN).astype(BF16)


def pick(name, source, index, with_copy, start=0, stop=None, begun=(), deps=()):
    seqs, _, routed = index.shape
    length, width = source.shape[0] // seqs, source.shape[1]
    whole_seq = pl.BlockSpec((length, width), lambda s: (s + start, 0))
    part = pl.BlockSpec((routed, width), lambda s: (s + start, 0))
    rows = shaped((seqs * routed, width), BF16)
    return call(
        functools.partial(begun_body, pick_cot_body if with_copy else pick_body, len(begun)),
        name,
        ((stop or seqs) - start,),
        [pl.BlockSpec((1, 1, routed), lambda s: (s + start, 0, 0)), whole_seq]
        + [pl.BlockSpec(memory_space=pl.ANY)] * len(begun),
        [part, whole_seq] if with_copy else part,
        [rows, shaped(source.shape, F32)] if with_copy else rows,
        flops=2 * seqs * routed * length * width,
        nbytes=6 * source.size,
        deps=deps,
        alias={2 + i: i for i in range(len(begun))},
    )(index, source, *begun)


def begun_body(body, count, index, source, *refs):
    body(index, source, *refs[count:])


def lay_rc(w, buf, kb):
    rs, cs, tall, wp = w.shape
    pieces = tall // kb
    for r in range(rs):
        for c in range(cs):
            for t in range(pieces):
                at = (c * pieces + t) * wp
                buf[r * kb : (r + 1) * kb, at : at + wp] = w[r, c, t * kb : (t + 1) * kb, :]


def lay_cr(w, buf, kb):
    rs, cs, tall, wp = w.shape
    pieces = tall // kb
    for r in range(rs):
        for c in range(cs):
            for t in range(pieces):
                at = (r * pieces + t) * wp
                buf[c * kb : (c + 1) * kb, at : at + wp] = w[r, c, t * kb : (t + 1) * kb, :]


def lay_turned(spots, own, other, place, rs, zs, looped=False):
    bit = spots[2, 0]
    for core in range(2):

        def lay(r, carry):
            for z in range(zs):
                place(r, z, core, own)
                place(r, z, 1 - core, other)
            return carry

        @pl.when(bit == core)
        def _():
            if looped:
                lax.fori_loop(0, rs, lay, 0)
            else:
                for r in range(rs):
                    lay(r, 0)


def project_body(
    kb, wp, count, spots, picked, grows, own_a, own_b, other_a, other_b, own_s, other_s,
    out, natural, normed, gmlp, gate, small,
):
    rs, zs = own_s.shape[:2]
    tall = kb * count // 2
    rows, width = picked.shape
    each = width // (rs * zs * 2)

    def place_small(r, z, core, source):
        at = (r * zs * 2 + 2 * z + core) * each
        line = source[spots[0, r], spots[3, z], 0:16, :].astype(F32)
        for k in range(3):
            small[k : k + 1, at : at + each] = line[0:1, k * each : (k + 1) * each]

    @pl.when(pl.program_id(0) == 0)
    def _():
        lay_turned(spots, own_s, other_s, place_small, rs, zs)
        chunk = 128

        def prepare(i, carry):
            at = pl.ds(pl.multiple_of(i * chunk, chunk), chunk)
            value = picked[at, :].astype(F32)
            opened = jax.nn.sigmoid(jnp.sum(value * small[0:1, :], axis=-1, keepdims=True))
            inverse = lax.rsqrt(jnp.mean(value * value, axis=-1, keepdims=True) + EPSILON)
            normed[at, :] = (value * inverse * small[1:2, :]).astype(BF16)
            gmlp[at, :] = (grows[at, :].astype(F32) * opened).astype(BF16)
            gate[at, :] = opened
            return carry

        lax.fori_loop(0, rows // chunk, prepare, 0)

    def place(r, z, core, halves_of):
        size = kb // 2
        for t in range(2 * count):
            half, at = divmod(t * size, tall)
            value = halves_of[half][spots[half, r], 0, at : at + size, :]
            lane = (core * count + t // 2) * wp
            down = pl.multiple_of(r * kb + t % 2 * size, size)
            natural[pl.ds(down, size), lane : lane + wp] = value

    lay_turned(spots, (own_a, own_b), (other_a, other_b), place, rs, 1, looped=True)
    out[...] = mul(normed[...], natural[...]).astype(BF16)


def project(spots, picked, grows, parts, kb, count):
    rows, depth = picked.shape
    rs, zs, tall, wp = parts[0].shape
    step = 2 * count * wp
    piece = pl.BlockSpec((rs, 1, tall, wp), lambda j, spots: (0, spots[3, j], 0, 0))
    last = pl.BlockSpec((rs, zs, 16, wp), lambda j, _: (0, 0, tall // 16 - 1, 0))
    return call(
        functools.partial(project_body, kb, wp, count),
        "project",
        (zs,),
        [whole(picked.shape)] * 2 + [piece] * 4 + [last] * 2,
        [
            pl.BlockSpec((rows, step), lambda j, _: (0, j)),
            pl.BlockSpec((depth, step), lambda j, _: (0, j)),
            whole(picked.shape),
            whole(picked.shape),
            whole((rows, 1)),
            whole((3, depth)),
        ],
        [
            shaped((rows, zs * step), BF16),
            shaped((depth, zs * step), BF16),
            shaped(picked.shape, BF16),
            shaped(picked.shape, BF16),
            shaped((rows, 1), F32),
            shaped((3, depth), F32),
        ],
        prefetch=1,
        flops=2 * rows * depth * zs * step,
        nbytes=2 * (4 * picked.size + 2 * depth * zs * step + rows * zs * step),
    )(spots, picked, grows, *parts, parts[0], parts[2])


def halves():
    lane = lax.broadcasted_iota(jnp.int32, (1, 2 * HD), 1)
    low = jnp.where(lane < HD, 1.0, 0.0).astype(BF16)
    high = jnp.where(lane < HD, 0.0, 1.0).astype(BF16)
    return low, high


def turned(x):
    return jnp.concatenate([x[:, HD:], x[:, :HD]], axis=1) * jnp.asarray(HD**-0.5, BF16)


def causal_of(routed):
    return lax.broadcasted_iota(jnp.int32, (routed, routed), 0) <= lax.broadcasted_iota(
        jnp.int32, (routed, routed), 1
    )


def attend_body(proj, context, probs):
    routed = proj.shape[0]
    low, high = halves()
    causal = causal_of(routed)
    tiles = [proj[:, i * 2 * HD : (i + 1) * 2 * HD] for i in range(3 * HEADS // 2)]
    scores = []
    for a, b, c in zip(tiles[::3], tiles[1::3], tiles[2::3]):
        scores.append(mul(turned(a) * low, a, NT))
        scores.append(mul(turned(c) * high, b, NT))
    scores = [jnp.where(causal, score, -1e30) for score in scores]
    highest = [jnp.max(score, axis=0, keepdims=True) for score in scores]
    expanded = [jnp.exp(score - top) for score, top in zip(scores, highest)]
    inverse = [1.0 / jnp.sum(e, axis=0, keepdims=True) for e in expanded]
    weights = [(e * i).astype(BF16) for e, i in zip(expanded, inverse)]
    for pair in range(HEADS // 2):
        b, c = tiles[3 * pair + 1], tiles[3 * pair + 2]
        both = jnp.concatenate(weights[2 * pair : 2 * pair + 2], axis=0)
        probs[0, 2 * pair * routed : 2 * (pair + 1) * routed, :] = both
        mixed = mul(both, jnp.concatenate([b * low, c * high], axis=0), TN)
        context[:, pair * 2 * HD : (pair + 1) * 2 * HD] = mixed.astype(BF16)


def attend(projected, seqs):
    rows, wide = projected.shape
    routed = rows // seqs
    width = wide // 3
    return call(
        attend_body,
        "attend",
        (seqs,),
        [pl.BlockSpec((routed, wide), lambda s: (s, 0))],
        [
            pl.BlockSpec((routed, width), lambda s: (s, 0)),
            pl.BlockSpec((1, HEADS * routed, routed), lambda s: (s, 0, 0)),
        ],
        [shaped((rows, width), BF16), shaped((seqs, HEADS * routed, routed), BF16)],
        flops=20 * rows * wide * routed,
        nbytes=8 * projected.size,
    )(projected)


def mix_body(kb, context, w, picked, gain, attn, normed, natural):
    @pl.when(pl.program_id(0) == 0)
    def _():
        lay_cr(w, natural, kb)

    out = mul(context[...], natural[...])
    attn[...] = out
    middle = picked[...].astype(F32) + out
    inverse = lax.rsqrt(jnp.mean(middle * middle, axis=-1, keepdims=True) + EPSILON)
    normed[...] = (middle * inverse * gain[...]).astype(BF16)


def mix(context, w, at, tall, kb, picked, gain, steps):
    rows, width = context.shape
    rs, cs, _, wp = w.shape
    part = pl.BlockSpec((rows // steps, width), lambda s: (s, 0))
    return call(
        functools.partial(mix_body, kb),
        "mix",
        (steps,),
        [part, pl.BlockSpec((rs, cs, tall, wp), lambda s: (0, 0, at, 0)), part, whole(gain.shape)],
        [part, part, whole((width, width))],
        [shaped((rows, width), F32), shaped((rows, width), BF16), shaped((width, width), BF16)],
        flops=2 * rows * width * width,
        nbytes=14 * rows * width,
    )(context, w, picked, gain)


GELU_A = 0.7978845608028654
GELU_B = 0.044715


def raise_body(kb, bit, x, gmlp, w, hidden, slope, natural, send, keep):
    lay_rc(w, natural, kb)
    rs, _, tall, wp = send.shape
    fb = hidden.shape[1] // 2

    def half_of(h, carry):
        across = pl.ds(pl.multiple_of(h * fb, fb), fb)
        pre = mul(x[...], natural[:, across])
        square = pre * pre
        half = 0.5 + 0.5 * jnp.tanh(pre * (GELU_A + (GELU_A * GELU_B) * square))
        value = pre * half
        hidden[:, across] = value.astype(BF16)
        slope[:, across] = (
            half + value * (1.0 - half) * (2 * GELU_A + (6 * GELU_A * GELU_B) * square)
        ).astype(BF16)
        total = mul(hidden[:, across], gmlp[...], TN).astype(BF16)
        many = tall // fb

        def put(target):
            for r in range(rs):
                for t in range(many):
                    lane = (r * many + t) * wp
                    target[r, 0, t * fb : (t + 1) * fb, :] = total[:, lane : lane + wp]

        @pl.when(bit[0] == h)
        def _():
            put(keep)

        @pl.when(bit[0] != h)
        def _():
            put(send)

        return carry

    lax.fori_loop(0, 2, half_of, 0)


def raised(bit, x, gmlp, w, at, tall, kb, shape):
    rows, depth = x.shape
    rs, cs, _, wp = w.shape
    fb = (tall // kb) * wp
    zs = cs // 2
    out = pl.BlockSpec((rows, 2 * fb), lambda j, _: (0, j))
    half = (rs, zs, shape[2] * shape[3] // wp, wp)
    grad = pl.BlockSpec((rs, 1) + half[2:], lambda j, _: (0, j, 0, 0))
    return call(
        functools.partial(raise_body, kb),
        "raise",
        (zs,),
        [once(x.shape), once(gmlp.shape)]
        + [pl.BlockSpec((rs, 2, tall, wp), lambda j, _: (0, j, at, 0))],
        [out, out, pl.BlockSpec((depth, 2 * fb), lambda j, _: (0, j)), grad, grad],
        [shaped((rows, cs * fb), BF16)] * 2
        + [shaped((depth, cs * fb), BF16)]
        + [shaped(half, BF16)] * 2,
        prefetch=1,
        flops=5 * rows * depth * cs * fb,
        nbytes=2 * (x.size + 3 * depth * cs * fb + 2 * rows * cs * fb),
    )(bit, x, gmlp, w)


def split_out(bit, first, second, keep, send, at):
    @pl.when(bit == 0)
    def _():
        keep[at] = first
        send[at] = second

    @pl.when(bit != 0)
    def _():
        keep[at] = second
        send[at] = first


def grad_rc(bit, total, send, keep, kb, nb):
    rs, zs, _, wp = send.shape
    for r in range(rs):
        for j in range(zs):
            for t in range(nb // wp):
                at = 2 * j * nb + t * wp
                down = slice(r * kb, (r + 1) * kb)
                where = (r, j, slice(t * kb, (t + 1) * kb))
                split_out(
                    bit, total[down, at : at + wp], total[down, at + nb : at + nb + wp], keep, send, where
                )


def grad_cr(bit, total, send, keep, kb, nb):
    rs, zs, _, wp = send.shape
    for r in range(rs):
        for j in range(zs):
            for t in range(nb // wp):
                across = slice(r * nb + t * wp, r * nb + (t + 1) * wp)
                where = (r, j, slice(t * kb, (t + 1) * kb))
                at = 2 * j * kb
                split_out(
                    bit, total[at : at + kb, across], total[at + kb : at + 2 * kb, across], keep, send, where
                )


def qkv_grad_body(
    kb, nb, bit, x, y, w, gsmall, gain, send, keep, little_send, little_keep, first
):
    step = pl.program_id(0)
    total = mul(x[...], y[...], TN)

    @pl.when(step == 0)
    def _():
        first[...] = jnp.zeros_like(first)

    first[...] += jnp.sum(total * w[...].astype(F32), axis=-1, keepdims=True)
    grad_rc(bit[0], total.astype(BF16), send, keep, kb, nb)

    @pl.when(step == pl.num_programs(0) - 1)
    def _():
        rs, zs, tall, wp = little_send.shape
        size = 128
        eye = lax.broadcasted_iota(jnp.int32, (size, size), 0) == lax.broadcasted_iota(
            jnp.int32, (size, size), 1
        )
        column = [first[i : i + size, :] for i in range(0, first.shape[0], size)]
        column = [jnp.sum(jnp.where(eye, part, 0.0), axis=0, keepdims=True) for part in column]
        lines = [gsmall[0:1, :], gsmall[1:2, :], jnp.concatenate(column, axis=1) / gain[...]]
        each = gain.shape[1] // (rs * zs * 2)

        def line_of(r, c):
            at = (r * zs * 2 + c) * each
            parts = [line[:, at : at + each] for line in lines]
            parts.append(jnp.zeros((1, wp - 3 * each), F32))
            return jnp.broadcast_to(jnp.concatenate(parts, axis=1), (tall, wp)).astype(BF16)

        for r in range(rs):
            for z in range(zs):
                pair = line_of(r, 2 * z), line_of(r, 2 * z + 1)
                split_out(bit[0], *pair, little_keep, little_send, (r, z))


def qkv_weight_grad(bit, x, y, w, gsmall, gain, shape, wp, count, deps=()):
    rows, depth = x.shape
    rs, cs, kb, nb = shape
    zs = cs // 2
    many = zs // count
    tall = kb * nb // wp
    step = 2 * many * nb
    out = pl.BlockSpec((rs, many, tall, wp), lambda j, _: (0, j, 0, 0))
    little = (rs, zs, 16, wp)
    return call(
        functools.partial(qkv_grad_body, kb, nb),
        "qkv_grad",
        (count,),
        [
            whole(x.shape),
            pl.BlockSpec((rows, step), lambda j, _: (0, j)),
            pl.BlockSpec((depth, step), lambda j, _: (0, j)),
            whole(gsmall.shape),
            whole(gain.shape),
        ],
        [out, out, whole(little), whole(little)],
        [shaped((rs, zs, tall, wp), BF16)] * 2 + [shaped(little, BF16)] * 2,
        [pltpu.VMEM((depth, 1), F32)],
        prefetch=1,
        flops=2 * rows * depth * cs * nb,
        nbytes=2 * (x.size + y.size + 2 * w.size),
        deps=deps,
    )(bit, x, y, w, gsmall, gain)


def feed_back_body(
    kb, ub, bit, grows, w, slope, hidden, gate, x, w_up,
    natural, dots, send, keep, total, x_turned,
):
    rs, _, tall, wp = w.shape
    pieces_up = kb // wp
    step = pl.program_id(0)
    lay_cr(w, natural, kb)

    @pl.when(step == 0)
    def _():
        x_turned[...] = x[...].T
        dots[...] = jnp.zeros_like(dots)
        total[...] = jnp.zeros_like(total)

    def half(h, carry):
        at = pl.ds(pl.multiple_of(h * kb, kb), kb)
        back = mul(grows[...], natural[at, :], NT)
        gpre = (back * gate[...] * slope[:, at].astype(F32)).astype(BF16)
        product = back * hidden[:, at].astype(F32)
        summed = product[:, :128]
        for n in range(1, kb // 128):
            summed = summed + product[:, n * 128 : (n + 1) * 128]
        dots[...] += summed
        part = mul(x_turned[...], gpre).astype(BF16)

        def put(target):
            for r in range(rs):
                for t in range(pieces_up):
                    value = part[r * ub : (r + 1) * ub, t * wp : (t + 1) * wp]
                    target[r, 0, t * ub : (t + 1) * ub, :] = value

        @pl.when(bit[0] == h)
        def _():
            put(keep)

        @pl.when(bit[0] != h)
        def _():
            put(send)

        total[...] += mul(gpre, w_up[:, at], NT)
        return carry

    lax.fori_loop(0, 2, half, 0)


def feed_back(bit, grows, w, slope, hidden, gate, x, w_up, kb, ub, deps=()):
    rows, width = grows.shape
    rs, cs, tall, wp = w.shape
    zs = cs // 2
    deep = hidden.shape[1]
    fb = 2 * kb
    cut = pl.BlockSpec((rows, fb), lambda j, _: (0, j))
    half = (rs, zs, ub * kb // wp, wp)
    grad = pl.BlockSpec((rs, 1) + half[2:], lambda j, _: (0, j, 0, 0))
    return call(
        functools.partial(feed_back_body, kb, ub),
        "feed_back",
        (zs,),
        [once(grows.shape), pl.BlockSpec((rs, 2, tall, wp), lambda j, _: (0, j, 0, 0)), cut, cut]
        + [once(gate.shape), once(x.shape), pl.BlockSpec((width, fb), lambda j, _: (0, j))],
        [
            pl.BlockSpec((fb, width), lambda j, _: (j, 0)),
            whole((rows, 128)),
            grad,
            grad,
            whole((rows, width)),
        ],
        [shaped((deep, width), BF16), shaped((rows, 128), F32)]
        + [shaped(half, BF16)] * 2
        + [shaped((rows, width), F32)],
        [pltpu.VMEM((width, rows), BF16)],
        prefetch=1,
        flops=6 * rows * width * deep,
        nbytes=2 * (3 * width * deep + 2 * rows * deep + 4 * rows * width),
        deps=deps,
    )(bit, grows, w, slope, hidden, gate, x, w_up)


def norm_back(grad, v, inverse, gain):
    scaled = grad * gain
    summed = jnp.sum(scaled * v, axis=-1, keepdims=True)
    return inverse * scaled - v * (inverse * inverse * inverse * summed / v.shape[-1])


def context_back_body(
    kb, nb, bit, total, attn, picked, grows, gate, dots, context, gain, w,
    gmid, gcontext, logit, gsmall, send, keep, gattn, gout,
):
    step = pl.program_id(0)

    @pl.when(step == 0)
    def _():
        gsmall[...] = jnp.zeros_like(gsmall)
        gout[...] = jnp.zeros_like(gout)

    chunk = 128

    def rows_back(i, carry):
        at = pl.ds(pl.multiple_of(i * chunk, chunk), chunk)
        grad = total[at, :]
        rows = picked[at, :].astype(F32)
        middle = rows + attn[at, :]
        inverse = lax.rsqrt(jnp.mean(middle * middle, axis=-1, keepdims=True) + EPSILON)
        gsmall[0:1, :] += jnp.sum(grad * middle * inverse, axis=0, keepdims=True)
        back = norm_back(grad, middle, inverse, gain[...])
        gmid[at, :] = back
        opened, dy = gate[at, :], grows[at, :].astype(F32)
        gattn[at, :] = (opened * dy + back).astype(BF16)
        opening = jnp.sum(dots[at, :], axis=-1, keepdims=True)
        opening += jnp.sum(dy * attn[at, :], axis=-1, keepdims=True)
        opening = opening * opened * (1.0 - opened)
        logit[at, :] = opening
        gsmall[1:2, :] += jnp.sum(opening * rows, axis=0, keepdims=True)
        return carry

    lax.fori_loop(0, total.shape[0] // chunk, rows_back, 0)
    gcontext[...] = mul(gattn[...], w[...], NT).astype(BF16)
    gout[...] += mul(context[...], gattn[...], TN)

    @pl.when(step == pl.num_programs(0) - 1)
    def _():
        grad_cr(bit[0], gout[...].astype(BF16), send, keep, kb, nb)


def context_back(bit, total, attn, picked, grows, gate, dots, context, gain, w, shape, wp, steps):
    rows, width = attn.shape
    rs, cs, kb, nb = shape
    half = (rs, cs // 2, kb * nb // wp, wp)
    size = rows // steps
    part = pl.BlockSpec((size, width), lambda j, _: (j, 0))
    thin = pl.BlockSpec((size, 1), lambda j, _: (j, 0))
    return call(
        functools.partial(context_back_body, kb, nb),
        "context_back",
        (steps,),
        [part] * 4
        + [thin, pl.BlockSpec((size, 128), lambda j, _: (j, 0)), part]
        + [once(gain.shape), once(w.shape)],
        [part, part, thin, whole((2, width)), whole(half), whole(half)],
        [
            shaped(attn.shape, F32),
            shaped(attn.shape, BF16),
            shaped(gate.shape, F32),
            shaped((2, width), F32),
            shaped(half, BF16),
            shaped(half, BF16),
        ],
        [pltpu.VMEM((size, width), BF16), pltpu.VMEM((width, width), F32)],
        prefetch=1,
        flops=4 * rows * width * width,
        nbytes=26 * rows * width + 6 * width * width,
    )(bit, total, attn, picked, grows, gate, dots, context, gain, w)


def attend_back_body(proj, gcontext, probs, out):
    routed = proj.shape[0]
    low, high = halves()
    tiles = [proj[:, i * 2 * HD : (i + 1) * 2 * HD] for i in range(3 * HEADS // 2)]
    grads, weights, grad_probs = [], [], []
    for pair in range(HEADS // 2):
        b, c = tiles[3 * pair + 1], tiles[3 * pair + 2]
        grad = gcontext[:, pair * 2 * HD : (pair + 1) * 2 * HD]
        grads += [grad * low, grad * high]
        for head in (2 * pair, 2 * pair + 1):
            weights.append(probs[0, head * routed : (head + 1) * routed, :])
        grad_probs += [mul(b, grads[-2], NT), mul(c, grads[-1], NT)]
    wide = [weight.astype(F32) for weight in weights]
    inner = [jnp.sum(g * w, axis=0, keepdims=True) for g, w in zip(grad_probs, wide)]
    backs = [(w * (g - i)).astype(BF16) for g, w, i in zip(grad_probs, wide, inner)]
    for pair in range(HEADS // 2):
        a, b, c = (turned(tile) for tile in tiles[3 * pair : 3 * pair + 3])
        (first, second), (low_grad, high_grad) = (
            each[2 * pair : 2 * pair + 2] for each in (backs, grads)
        )
        at = [slice((3 * pair + t) * 2 * HD, (3 * pair + t + 1) * 2 * HD) for t in range(3)]
        out[:, at[0]] = (mul(first, a * low, TN) + mul(first, a * high)).astype(BF16)
        out[:, at[1]] = (mul(weights[2 * pair], low_grad) + mul(second, c * high, TN)).astype(BF16)
        left = jnp.concatenate([second, weights[2 * pair + 1]], axis=1)
        right = jnp.concatenate([b * low, high_grad], axis=0)
        out[:, at[2]] = mul(left, right).astype(BF16)


def attend_back(projected, gcontext, probs, seqs, deps=()):
    rows, wide = projected.shape
    routed = rows // seqs
    return call(
        attend_back_body,
        "attend_back",
        (seqs,),
        [
            pl.BlockSpec((routed, wide), lambda s: (s, 0)),
            pl.BlockSpec((routed, wide // 3), lambda s: (s, 0)),
            pl.BlockSpec((1, HEADS * routed, routed), lambda s: (s, 0, 0)),
        ],
        pl.BlockSpec((routed, wide), lambda s: (s, 0)),
        shaped((rows, wide), BF16),
        flops=40 * rows * wide * routed,
        nbytes=16 * projected.size,
        deps=deps,
    )(projected, gcontext, probs)


def picked_back_body(
    places, gproj, w, logit, gain, router, picked, gmid, grows, base,
    out, total, picked_in, gmid_in, grows_in, fetched, arrived,
):
    j = pl.program_id(0)
    step = w.shape[0]
    loads = [
        pltpu.make_async_copy(source, target, fetched.at[i])
        for i, (source, target) in enumerate(
            ((picked, picked_in), (gmid, gmid_in), (grows, grows_in))
        )
    ]

    @pl.when(j == 0)
    def _():
        for load in loads:
            load.start()

    total[j] = mul(gproj[...], w[...], NT)

    @pl.when(j == pl.num_programs(0) - 1)
    def _():
        for load in loads:
            load.wait()
        chunk = 128
        count = total.shape[1] // chunk

        def compute(i):
            at = pl.ds(pl.multiple_of(i * chunk, chunk), chunk)
            grad = jnp.concatenate([total[n, at, :] for n in range(total.shape[0])], axis=1)
            rows = picked_in[at, :].astype(F32)
            inverse = lax.rsqrt(jnp.mean(rows * rows, axis=-1, keepdims=True) + EPSILON)
            back = norm_back(grad, rows, inverse, gain[...])
            gmid_in[at, :] = (
                gmid_in[at, :]
                + back
                + (logit[at, :] * router[...] + grows_in[at, :].astype(F32))
            )

        def copy(row):
            pltpu.make_async_copy(
                gmid_in.at[pl.ds(row, 1)], out.at[pl.ds(places[row], 1)], arrived
            ).start()

        def both(i, carry):
            for k in range(chunk):
                copy((i - 1) * chunk + k)
            compute(i)
            return carry

        def last(row, carry):
            copy(row)
            return carry

        compute(0)
        lax.fori_loop(1, count, both, 0)
        lax.fori_loop((count - 1) * chunk, count * chunk, last, 0, unroll=8)
        pltpu.make_async_copy(gmid_in, out.at[pl.ds(0, gmid_in.shape[0])], arrived).wait()


def picked_back(places, gproj, w, picked, gmid, logit, grows, gain, router, base, step, deps=()):
    rows, deep = gproj.shape
    width = picked.shape[1]
    return call(
        picked_back_body,
        "picked_back",
        (width // step,),
        [once(gproj.shape), pl.BlockSpec((step, deep), lambda j, _: (j, 0))]
        + [once(t.shape) for t in (logit, gain, router)]
        + [pl.BlockSpec(memory_space=pl.ANY)] * 4,
        pl.BlockSpec(memory_space=pl.ANY),
        shaped(base.shape, F32),
        [
            pltpu.VMEM((width // step, rows, step), F32),
            pltpu.VMEM((rows, width), BF16),
            pltpu.VMEM((rows, width), F32),
            pltpu.VMEM((rows, width), BF16),
            pltpu.SemaphoreType.DMA((3,)),
            pltpu.SemaphoreType.DMA,
        ],
        prefetch=1,
        flops=2 * rows * deep * width,
        nbytes=2 * (gproj.size + w.size) + 10 * picked.size,
        alias={9: 0},
        deps=deps,
    )(places, gproj, w, logit, gain, router, picked, gmid, grows, base)


def join_body(count, *refs):
    out, at = refs[-1], 0
    for keep, got in zip(refs[:count], refs[count : 2 * count]):
        tall = keep.shape[2]

        def add(z, carry):
            total = keep[0, z].astype(F32) + got[0, z].astype(F32)
            out[0, z, at : at + tall, :] = total.astype(BF16)
            return carry

        lax.fori_loop(0, keep.shape[1], add, 0)
        at += tall


def joined(keeps, gots, deps=()):
    rs, zs, _, wp = keeps[0].shape
    talls = [k.shape[2] for k in keeps]
    blocks = [pl.BlockSpec((1, zs, tall, wp), lambda r: (r, 0, 0, 0)) for tall in talls]
    tall = sum(talls)
    return call(
        functools.partial(join_body, len(keeps)),
        "join",
        (rs,),
        blocks * 2,
        pl.BlockSpec((1, zs, tall, wp), lambda r: (r, 0, 0, 0)),
        shaped((rs, zs, tall, wp), BF16),
        flops=rs * zs * tall * wp,
        nbytes=6 * rs * zs * tall * wp,
        vmem=16,
        deps=deps,
    )(*keeps, *gots)


def lower_body(hidden, w, attn, picked, gate, kept):
    branch = attn[...] + mul(hidden[...], w[...])
    kept[...] = (picked[...].astype(F32) + gate[...] * branch).astype(BF16)


def lowered(hidden, w, attn, picked, gate, step, deps=()):
    rows, deep = hidden.shape
    width = w.shape[1]
    cut = pl.BlockSpec((rows, step), lambda j: (0, j))
    return call(
        lower_body,
        "lower",
        (width // step,),
        [whole(hidden.shape), pl.BlockSpec((deep, step), lambda j: (0, j))]
        + [cut] * 2
        + [whole(gate.shape)],
        cut,
        shaped((rows, width), BF16),
        flops=2 * rows * deep * width,
        nbytes=2 * (hidden.size + w.size) + 8 * attn.size,
        deps=deps,
    )(hidden, w, attn, picked, gate)


def place_body(index, tok, kept, output):
    found = one_hot(index, tok.shape[0])
    hot = jnp.where(found, 1.0, 0.0)
    routed = jnp.sum(hot, axis=-1, keepdims=True) > 0.5
    output[...] = jnp.where(
        routed, mul(hot.astype(BF16), kept[...]), tok[...].astype(F32)
    ).astype(BF16)


def place(tokens, index, kept, deps=()):
    seqs, _, routed = index.shape
    length, width = tokens.shape[0] // seqs, tokens.shape[1]
    whole_seq = pl.BlockSpec((length, width), lambda s: (s, 0))
    return call(
        place_body,
        "place",
        (seqs,),
        [
            pl.BlockSpec((1, 1, routed), lambda s: (s, 0, 0)),
            whole_seq,
            pl.BlockSpec((routed, width), lambda s: (s, 0)),
        ],
        whole_seq,
        shaped(tokens.shape, BF16),
        flops=2 * seqs * routed * length * width,
        nbytes=4 * tokens.size,
        deps=deps,
    )(index, tokens, kept)


def pieces_body(qkv, out, up, down, small, first, second, third):
    def lay(target, at, block):
        kb, nb = block.shape
        wp = target.shape[1]
        for t in range(nb // wp):
            target[at + t * kb : at + (t + 1) * kb, :] = block[:, t * wp : (t + 1) * wp]

    kb, nb = qkv.shape
    wp = first.shape[1]
    size = kb // 2
    middle = kb * nb // wp // 2
    for t in range(2 * nb // wp):
        at = t * size + (16 if t * size >= middle else 0)
        value = qkv[t % 2 * size : (t % 2 + 1) * size, t // 2 * wp : (t // 2 + 1) * wp]
        first[at : at + size, :] = value
    first[middle : middle + 16, :] = small[...]
    first[2 * middle + 16 :, :] = jnp.zeros_like(small)
    lay(second, 0, up)
    lay(second, up.shape[0] * up.shape[1] // wp, out)
    lay(third, 0, down)


def pieces(qkv, out, up, down, small):
    wp = small.shape[1]
    talls = (qkv.size // wp + 32, (up.size + out.size) // wp, down.size // wp)
    return call(
        pieces_body,
        "pieces",
        (1,),
        [whole(w.shape) for w in (qkv, out, up, down, small)],
        [whole((tall, wp)) for tall in talls],
        [shaped((tall, wp), BF16) for tall in talls],
        nbytes=4 * sum(talls) * wp,
        vmem=60,
    )(qkv, out, up, down, small)


def gathered(flat, rs, cs):
    return lax.all_gather(flat, BOTH, axis=0, tiled=True).reshape(rs, cs, *flat.shape)


def shifted(value, part, shift, rs, cs):
    side = math.isqrt(rs)
    if part == "x":
        moves = [(r, r // side * side + (r + shift) % side) for r in range(rs)]
    elif part == "y":
        moves = [(r, (r + shift * side) % rs) for r in range(rs)]
    else:
        moves = [(c, (c + 2 * shift) % cs) for c in range(cs)]
    return lax.ppermute(value, "col" if part == "z" else "row", moves)


def permuted(flat, rs, cs, during):
    side, zs = math.isqrt(rs), cs // 2
    line = [flat] + [shifted(flat, "z", i, rs, cs) for i in range(1, zs)]
    line[0] = tied(flat, during[0])
    tall = flat.shape[0] // 2
    held = [jnp.stack([part[h * tall : (h + 1) * tall] for part in line])[None] for h in range(2)]
    for order in ("xy", "yx"):
        moved = [
            [shifted(h, part, i, rs, cs) for i in range(1, side)] for h, part in zip(held, order)
        ]
        if order == "xy":
            done, result = during[1](held[0])
        else:
            done, result = during[2](held[0], result)
        held[0] = tied(held[0], done)
        held = [jnp.concatenate([h] + m) for h, m in zip(held, moved)]
    pairs = [(c, c ^ 1) for c in range(cs)]
    return held + [lax.ppermute(h, "col", pairs) for h in held], result


def spots_of(rs, cs):
    side, zs = math.isqrt(rs), cs // 2
    row, column = lax.axis_index("row"), lax.axis_index("col")
    r, z = jnp.arange(rs), jnp.arange(zs)
    y, x = (row // side - r // side) % side, (row - r) % side
    table = jnp.zeros((4, max(rs, zs)), jnp.int32)
    table = table.at[0, :rs].set(y * side + x).at[1, :rs].set(x * side + y)
    return table.at[2, :].set(column % 2).at[3, :zs].set((column // 2 - z) % zs)


def local(
    tokens,
    router_weight,
    norm_first,
    qkv_weight,
    out_weight,
    norm_second,
    up_weight,
    down_weight,
    route_index,
    out_cotangent,
    rs,
    cs,
):
    seqs, routed = route_index.shape
    width = tokens.shape[1]
    index = route_index.reshape(seqs, 1, routed)
    column = lax.axis_index("col")
    core, depth = column % 2, column // 2
    zs = cs // 2
    bit = core.astype(jnp.int32).reshape(1)
    pairs = [(c, c ^ 1) for c in range(cs)]
    blocks = [w.shape for w in (qkv_weight, out_weight, up_weight, down_weight)]
    shape_qkv, shape_out, shape_up, shape_down = ((rs, cs) + b for b in blocks)
    wp = math.gcd(128, *(b[1] for b in blocks))
    tall_qkv, tall_out, tall_up, tall_down = (b[0] * b[1] // wp for b in blocks)

    spots = spots_of(rs, cs)
    small = jnp.concatenate([router_weight, norm_first, norm_second])
    small = jnp.pad(small.reshape(1, -1), ((0, 15), (0, wp - small.shape[0])))
    flat, next_flat, down_flat = pieces(qkv_weight, out_weight, up_weight, down_weight, small)

    def pick_first(dep):
        result = pick("pick_first", out_cotangent, index, True, 0, seqs // 3, deps=(dep,))
        return result[0], result

    def pick_rest(dep, begun):
        result = pick("pick_rest", out_cotangent, index, True, seqs // 3, None, begun, deps=(dep,))
        return result[0], result

    picked = pick("pick", tokens, index, False)
    parts, (grows, base) = permuted(flat, rs, cs, (picked, pick_first, pick_rest))
    next_parts = gathered(next_flat, rs, cs)
    down_parts = gathered(down_flat, rs, cs)

    def exchanged(send):
        return lax.ppermute(send, "col", pairs)

    def by_row(keep):
        r, z, tall, _ = keep.shape
        mine = lax.psum_scatter(
            keep.reshape(r * z * tall, wp), "row", scatter_dimension=0, tiled=True
        )
        return mine.reshape(z, tall, wp)

    def depth_parts(mine):
        return [
            lax.dynamic_index_in_dim(mine, (depth + shift) % zs, 0, keepdims=False)
            for shift in range(zs)
        ]

    def depth_sum(parts, *deps):
        total = (tied(parts[0], *deps) if deps else parts[0]).astype(F32)
        for shift in range(1, zs):
            total = total + shifted(parts[shift], "z", shift, rs, cs).astype(F32)
        return total

    def block(total, shape):
        kb, nb = shape[2:]
        return jnp.concatenate([total[i : i + kb] for i in range(0, kb * nb // wp, kb)], axis=1)

    projected, w_qkv, normed, gmlp, gate, small = project(
        spots, picked, grows, parts, blocks[0][0], blocks[0][1] // wp
    )
    router, first_gain, second_gain = small[0:1], small[1:2], small[2:3]
    context, probs = attend(projected, seqs)
    attn, normed_mid, w_out = mix(
        context, next_parts, tall_up // tall_out, tall_out, blocks[1][0], picked, second_gain, 3
    )
    hidden, slope, w_up, down_send, down_keep = raised(
        bit, normed_mid, gmlp, next_parts, 0, tall_up, blocks[2][0], shape_down
    )
    down_keep = joined([down_keep], [exchanged(down_send)])
    down_rows = by_row(down_keep)

    w_down, dots, up_send, up_keep, gnormed = feed_back(
        bit, grows, down_parts, slope, hidden, gate, normed_mid, w_up,
        blocks[3][0], blocks[2][0], deps=(down_keep,),
    )
    gmid, gcontext, logit, gsmall, out_send, out_keep = context_back(
        bit, gnormed, attn, picked, grows, gate, dots, context, second_gain, w_out, shape_out, wp, 3
    )
    up_keep = joined(
        [up_keep, out_keep], [exchanged(up_send), exchanged(out_send)], deps=(gcontext,)
    )
    up_rows = by_row(up_keep)
    down_sums = depth_parts(down_rows)

    gproj = attend_back(projected, gcontext, probs, seqs, deps=(up_keep, *down_sums))
    down_total = depth_sum(down_sums, gproj)
    qkv_send, qkv_keep, little_send, little_keep = qkv_weight_grad(
        bit, normed, gproj, w_qkv, gsmall, first_gain, shape_qkv, wp, 4, deps=(down_total,)
    )
    qkv_keep = joined(
        [qkv_keep, little_keep], [exchanged(qkv_send), exchanged(little_send)]
    )
    qkv_rows = by_row(qkv_keep)

    up_parts = depth_parts(up_rows)
    starts = jnp.arange(seqs, dtype=jnp.int32) * (tokens.shape[0] // seqs)
    places = (route_index + starts[:, None]).reshape(-1)
    input_grad = picked_back(
        places, gproj, w_qkv, picked, gmid, logit, grows, first_gain, router, base, 256,
        deps=(qkv_keep, *up_parts),
    )
    kept = lowered(hidden, w_down, attn, picked, gate, 256, deps=(input_grad,))
    up_total = depth_sum(up_parts, kept)
    qkv_parts = depth_parts(qkv_rows)
    output = place(tokens, index, kept, deps=(up_total, *qkv_parts))
    down_grad, up_grad = block(down_total, shape_down), block(up_total[:tall_up], shape_up)
    qkv_total = depth_sum(qkv_parts, output)
    out_grad = block(up_total[tall_up:], shape_out)
    qkv_grad = block(qkv_total[:tall_qkv], shape_qkv)
    sums = qkv_total[tall_qkv, : 3 * width // (rs * cs)].reshape(3, -1)
    return (
        output,
        input_grad,
        sums[1],
        sums[2],
        qkv_grad,
        out_grad,
        sums[0],
        up_grad,
        down_grad,
    )


def solution(mesh):
    both, by_row, by_col = P(BOTH), P("row", "col"), P("col", "row")
    tall = P(BOTH, None)
    return jax.shard_map(
        functools.partial(local, rs=mesh.shape["row"], cs=mesh.shape["col"]),
        mesh=mesh,
        in_specs=(tall, both, both, by_row, by_col, both, by_row, by_col, tall, tall),
        out_specs=(tall, tall, both, both, by_row, by_col, both, by_row, by_col),
        check_vma=False,
    )
```

```python
import functools
import math

import jax
import jax.numpy as jnp
from jax import lax
from jax.experimental import pallas as pl
from jax.experimental.pallas import tpu as pltpu
from jax.sharding import PartitionSpec as P

HEADS = 16
HD = 64
EPSILON = 1e-06
F32 = jnp.float32
BF16 = jnp.bfloat16
BOTH = ("row", "col")
SLOW = 1

NN = (((1,), (0,)), ((), ()))
NT = (((1,), (1,)), ((), ()))
TN = (((0,), (0,)), ((), ()))


def mul(a, b, dims=NN):
    return lax.dot_general(a, b, dims, preferred_element_type=F32)


def call(
    body, name, grid, ins, outs, shapes, scratch=(), prefetch=0, flops=0, nbytes=0, deps=(), alias=None, vmem=56
):
    count = prefetch + len(ins)

    def run(*refs):
        body(*refs[:count], *refs[count + len(deps) :])

    made = pl.pallas_call(
        run,
        name=name,
        grid_spec=pltpu.PrefetchScalarGridSpec(
            num_scalar_prefetch=prefetch,
            grid=grid,
            in_specs=ins + [pl.BlockSpec(memory_space=pl.ANY)] * len(deps),
            out_specs=outs,
            scratch_shapes=list(scratch),
        ),
        out_shape=shapes,
        input_output_aliases=alias or {},
        compiler_params=pltpu.CompilerParams(
            dimension_semantics=("arbitrary",) * len(grid),
            vmem_limit_bytes=vmem * 2**20,
        ),
        cost_estimate=pl.CostEstimate(
            flops=flops // SLOW, transcendentals=0, bytes_accessed=nbytes // SLOW
        ),
    )
    return lambda *args: made(*args, *deps)


def tied(value, *deps):
    return call(
        lambda given, out: None,
        "tied",
        (1,),
        [pl.BlockSpec(memory_space=pl.ANY)],
        pl.BlockSpec(memory_space=pl.ANY),
        shaped(value.shape, value.dtype),
        deps=deps,
        alias={0: 0},
        vmem=60,
    )(value)


def whole(shape):
    return pl.BlockSpec(shape, lambda *_: (0,) * len(shape))


def once(shape):
    return pl.BlockSpec(shape, lambda *_: (0,) * len(shape), pipeline_mode=pl.Buffered(1))


def shaped(shape, dtype):
    return jax.ShapeDtypeStruct(shape, dtype)


def one_hot(index_ref, length):
    places = lax.broadcasted_iota(jnp.int32, (length, index_ref.shape[-1]), 0)
    return places == index_ref[0]


def pick_cot_body(index, cot, grows, base):
    hot = jnp.where(one_hot(index, cot.shape[0]), 1.0, 0.0).astype(BF16)
    grows[...] = mul(hot, cot[...], TN).astype(BF16)
    base[...] = cot[...].astype(F32)


def pick_body(index, tok, picked):
    hot = jnp.where(one_hot(index, tok.shape[0]), 1.0, 0.0).astype(BF16)
    picked[...] = mul(hot, tok[...], TN).astype(BF16)


def pick(name, source, index, with_copy, start=0, stop=None, begun=(), deps=()):
    seqs, _, routed = index.shape
    length, width = source.shape[0] // seqs, source.shape[1]
    whole_seq = pl.BlockSpec((length, width), lambda s: (s + start, 0))
    part = pl.BlockSpec((routed, width), lambda s: (s + start, 0))
    rows = shaped((seqs * routed, width), BF16)
    return call(
        functools.partial(begun_body, pick_cot_body if with_copy else pick_body, len(begun)),
        name,
        ((stop or seqs) - start,),
        [pl.BlockSpec((1, 1, routed), lambda s: (s + start, 0, 0)), whole_seq]
        + [pl.BlockSpec(memory_space=pl.ANY)] * len(begun),
        [part, whole_seq] if with_copy else part,
        [rows, shaped(source.shape, F32)] if with_copy else rows,
        flops=2 * seqs * routed * length * width,
        nbytes=6 * source.size,
        deps=deps,
        alias={2 + i: i for i in range(len(begun))},
    )(index, source, *begun)


def begun_body(body, count, index, source, *refs):
    body(index, source, *refs[count:])


def lay_rc(w, buf, kb):
    rs, cs, tall, wp = w.shape
    pieces = tall // kb
    for r in range(rs):
        for c in range(cs):
            for t in range(pieces):
                at = (c * pieces + t) * wp
                buf[r * kb : (r + 1) * kb, at : at + wp] = w[r, c, t * kb : (t + 1) * kb, :]


def lay_cr(w, buf, kb):
    rs, cs, tall, wp = w.shape
    pieces = tall // kb
    for r in range(rs):
        for c in range(cs):
            for t in range(pieces):
                at = (r * pieces + t) * wp
                buf[c * kb : (c + 1) * kb, at : at + wp] = w[r, c, t * kb : (t + 1) * kb, :]


def lay_turned(spots, own, other, place, rs, zs, looped=False):
    bit = spots[2, 0]
    for core in range(2):

        def lay(r, carry):
            for z in range(zs):
                place(r, z, core, own)
                place(r, z, 1 - core, other)
            return carry

        @pl.when(bit == core)
        def _():
            if looped:
                lax.fori_loop(0, rs, lay, 0)
            else:
                for r in range(rs):
                    lay(r, 0)


def project_body(
    kb, wp, count, spots, picked, grows, own_a, own_b, other_a, other_b, own_s, other_s,
    out, natural, normed_turned, gmlp, gate, small, normed,
):
    rs, zs = own_s.shape[:2]
    tall = kb * count // 2
    rows, width = picked.shape
    each = width // (rs * zs * 2)

    def place_small(r, z, core, source):
        at = (r * zs * 2 + 2 * z + core) * each
        line = source[spots[0, r], spots[3, z], 0:16, :].astype(F32)
        for k in range(3):
            small[k : k + 1, at : at + each] = line[0:1, k * each : (k + 1) * each]

    @pl.when(pl.program_id(0) == 0)
    def _():
        lay_turned(spots, own_s, other_s, place_small, rs, zs)
        chunk = 128

        def prepare(i, carry):
            at = pl.ds(pl.multiple_of(i * chunk, chunk), chunk)
            value = picked[at, :].astype(F32)
            opened = jax.nn.sigmoid(jnp.sum(value * small[0:1, :], axis=-1, keepdims=True))
            inverse = lax.rsqrt(jnp.mean(value * value, axis=-1, keepdims=True) + EPSILON)
            scaled = (value * inverse * small[1:2, :]).astype(BF16)
            normed[at, :] = scaled
            normed_turned[:, at] = scaled.T
            gmlp[at, :] = (grows[at, :].astype(F32) * opened).astype(BF16)
            gate[at, :] = opened
            return carry

        lax.fori_loop(0, rows // chunk, prepare, 0)

    def place(r, z, core, halves_of):
        size = kb // 2
        for t in range(2 * count):
            half, at = divmod(t * size, tall)
            value = halves_of[half][spots[half, r], 0, at : at + size, :]
            lane = (core * count + t // 2) * wp
            down = pl.multiple_of(r * kb + t % 2 * size, size)
            natural[pl.ds(down, size), lane : lane + wp] = value

    lay_turned(spots, (own_a, own_b), (other_a, other_b), place, rs, 1, looped=True)
    out[...] = mul(normed[...], natural[...]).astype(BF16)


def project(spots, picked, grows, parts, kb, count):
    rows, depth = picked.shape
    rs, zs, tall, wp = parts[0].shape
    step = 2 * count * wp
    piece = pl.BlockSpec((rs, 1, tall, wp), lambda j, spots: (0, spots[3, j], 0, 0))
    last = pl.BlockSpec((rs, zs, 16, wp), lambda j, _: (0, 0, tall // 16 - 1, 0))
    return call(
        functools.partial(project_body, kb, wp, count),
        "project",
        (zs,),
        [whole(picked.shape)] * 2 + [piece] * 4 + [last] * 2,
        [
            pl.BlockSpec((rows, step), lambda j, _: (0, j)),
            pl.BlockSpec((depth, step), lambda j, _: (0, j)),
            whole((depth, rows)),
            whole(picked.shape),
            whole((rows, 1)),
            whole((3, depth)),
        ],
        [
            shaped((rows, zs * step), BF16),
            shaped((depth, zs * step), BF16),
            shaped((depth, rows), BF16),
            shaped(picked.shape, BF16),
            shaped((rows, 1), F32),
            shaped((3, depth), F32),
        ],
        [pltpu.VMEM((rows, depth), BF16)],
        prefetch=1,
        flops=2 * rows * depth * zs * step,
        nbytes=2 * (4 * picked.size + 2 * depth * zs * step + rows * zs * step),
    )(spots, picked, grows, *parts, parts[0], parts[2])


def halves():
    lane = lax.broadcasted_iota(jnp.int32, (1, 2 * HD), 1)
    low = jnp.where(lane < HD, 1.0, 0.0).astype(BF16)
    high = jnp.where(lane < HD, 0.0, 1.0).astype(BF16)
    return low, high


def turned(x):
    return jnp.concatenate([x[:, HD:], x[:, :HD]], axis=1) * jnp.asarray(HD**-0.5, BF16)


def causal_of(routed):
    return lax.broadcasted_iota(jnp.int32, (routed, routed), 0) <= lax.broadcasted_iota(
        jnp.int32, (routed, routed), 1
    )


def attend_body(proj, context, probs):
    routed = proj.shape[0]
    low, high = halves()
    causal = causal_of(routed)
    tiles = [proj[:, i * 2 * HD : (i + 1) * 2 * HD] for i in range(3 * HEADS // 2)]
    scores = []
    for a, b, c in zip(tiles[::3], tiles[1::3], tiles[2::3]):
        scores.append(mul(turned(a) * low, a, NT))
        scores.append(mul(turned(c) * high, b, NT))
    scores = [jnp.where(causal, score, -1e30) for score in scores]
    highest = [jnp.max(score, axis=0, keepdims=True) for score in scores]
    expanded = [jnp.exp(score - top) for score, top in zip(scores, highest)]
    inverse = [1.0 / jnp.sum(e, axis=0, keepdims=True) for e in expanded]
    weights = [(e * i).astype(BF16) for e, i in zip(expanded, inverse)]
    for pair in range(HEADS // 2):
        b, c = tiles[3 * pair + 1], tiles[3 * pair + 2]
        both = jnp.concatenate(weights[2 * pair : 2 * pair + 2], axis=0)
        probs[0, 2 * pair * routed : 2 * (pair + 1) * routed, :] = both
        mixed = mul(both, jnp.concatenate([b * low, c * high], axis=0), TN)
        context[:, pair * 2 * HD : (pair + 1) * 2 * HD] = mixed.astype(BF16)


def attend(projected, seqs):
    rows, wide = projected.shape
    routed = rows // seqs
    width = wide // 3
    return call(
        attend_body,
        "attend",
        (seqs,),
        [pl.BlockSpec((routed, wide), lambda s: (s, 0))],
        [
            pl.BlockSpec((routed, width), lambda s: (s, 0)),
            pl.BlockSpec((1, HEADS * routed, routed), lambda s: (s, 0, 0)),
        ],
        [shaped((rows, width), BF16), shaped((seqs, HEADS * routed, routed), BF16)],
        flops=20 * rows * wide * routed,
        nbytes=8 * projected.size,
    )(projected)


def mix_body(kb, context, w, picked, gain, attn, normed, turned_out, natural):
    @pl.when(pl.program_id(0) == 0)
    def _():
        lay_cr(w, natural, kb)

    out = mul(context[...], natural[...])
    attn[...] = out
    middle = picked[...].astype(F32) + out
    inverse = lax.rsqrt(jnp.mean(middle * middle, axis=-1, keepdims=True) + EPSILON)
    value = (middle * inverse * gain[...]).astype(BF16)
    normed[...] = value
    turned_out[...] = value.T


def mix(context, w, at, tall, kb, picked, gain, steps):
    rows, width = context.shape
    rs, cs, _, wp = w.shape
    part = pl.BlockSpec((rows // steps, width), lambda s: (s, 0))
    return call(
        functools.partial(mix_body, kb),
        "mix",
        (steps,),
        [part, pl.BlockSpec((rs, cs, tall, wp), lambda s: (0, 0, at, 0)), part, whole(gain.shape)],
        [part, part, pl.BlockSpec((width, rows // steps), lambda s: (0, s)), whole((width, width))],
        [
            shaped((rows, width), F32),
            shaped((rows, width), BF16),
            shaped((width, rows), BF16),
            shaped((width, width), BF16),
        ],
        flops=2 * rows * width * width,
        nbytes=14 * rows * width,
    )(context, w, picked, gain)


GELU_A = 0.7978845608028654
GELU_B = 0.044715


def raise_body(kb, bit, x, gmlp, w, hidden, slope, natural, send, keep):
    lay_rc(w, natural, kb)
    rs, _, tall, wp = send.shape
    fb = hidden.shape[1] // 2

    def half_of(h, carry):
        across = pl.ds(pl.multiple_of(h * fb, fb), fb)
        pre = mul(x[...], natural[:, across])
        square = pre * pre
        half = 0.5 + 0.5 * jnp.tanh(pre * (GELU_A + (GELU_A * GELU_B) * square))
        value = pre * half
        hidden[:, across] = value.astype(BF16)
        slope[:, across] = (
            half + value * (1.0 - half) * (2 * GELU_A + (6 * GELU_A * GELU_B) * square)
        ).astype(BF16)
        total = mul(hidden[:, across], gmlp[...], TN).astype(BF16)
        many = tall // fb

        def put(target):
            for r in range(rs):
                for t in range(many):
                    lane = (r * many + t) * wp
                    target[r, 0, t * fb : (t + 1) * fb, :] = total[:, lane : lane + wp]

        @pl.when(bit[0] == h)
        def _():
            put(keep)

        @pl.when(bit[0] != h)
        def _():
            put(send)

        return carry

    lax.fori_loop(0, 2, half_of, 0)


def raised(bit, x, gmlp, w, at, tall, kb, shape):
    rows, depth = x.shape
    rs, cs, _, wp = w.shape
    fb = (tall // kb) * wp
    zs = cs // 2
    out = pl.BlockSpec((rows, 2 * fb), lambda j, _: (0, j))
    half = (rs, zs, shape[2] * shape[3] // wp, wp)
    grad = pl.BlockSpec((rs, 1) + half[2:], lambda j, _: (0, j, 0, 0))
    return call(
        functools.partial(raise_body, kb),
        "raise",
        (zs,),
        [once(x.shape), once(gmlp.shape)]
        + [pl.BlockSpec((rs, 2, tall, wp), lambda j, _: (0, j, at, 0))],
        [out, out, pl.BlockSpec((depth, 2 * fb), lambda j, _: (0, j)), grad, grad],
        [shaped((rows, cs * fb), BF16)] * 2
        + [shaped((depth, cs * fb), BF16)]
        + [shaped(half, BF16)] * 2,
        prefetch=1,
        flops=5 * rows * depth * cs * fb,
        nbytes=2 * (x.size + 3 * depth * cs * fb + 2 * rows * cs * fb),
    )(bit, x, gmlp, w)


def split_out(bit, first, second, keep, send, at):
    @pl.when(bit == 0)
    def _():
        keep[at] = first
        send[at] = second

    @pl.when(bit != 0)
    def _():
        keep[at] = second
        send[at] = first


def grad_cr(bit, total, send, keep, kb, nb):
    rs, zs, _, wp = send.shape
    for r in range(rs):
        for j in range(zs):
            for t in range(nb // wp):
                across = slice(r * nb + t * wp, r * nb + (t + 1) * wp)
                where = (r, j, slice(t * kb, (t + 1) * kb))
                at = 2 * j * kb
                split_out(
                    bit, total[at : at + kb, across], total[at + kb : at + 2 * kb, across], keep, send, where
                )


def qkv_grad_body(kb, nb, last, many, bit, x, *refs):
    y, w, refs = refs[:many], refs[many : 2 * many], refs[2 * many :]
    if last:
        gsmall, gain, before, out, little_send, little_keep, first, columns, weights = refs
    else:
        out, first, columns, weights = refs
    step = pl.program_id(0)
    rs, zs, _, wp = out.shape
    side_here = bit[0] if last else 1 - bit[0]
    if many > 1:
        for j in range(zs):
            columns[:, j * nb : (j + 1) * nb] = y[j][...]
            weights[:, j * nb : (j + 1) * nb] = w[j][...]
    else:
        for side in range(2):

            @pl.when(side_here == side)
            def _():
                for j in range(zs):
                    source = slice((2 * j + side) * nb, (2 * j + side + 1) * nb)
                    target = slice(j * nb, (j + 1) * nb)
                    columns[:, target] = y[0][:, source]
                    weights[:, target] = w[0][:, source]

    @pl.when(step == 0)
    def _():
        first[...] = before[...] if last else jnp.zeros_like(first)

    total = mul(x[...], columns[...])
    first[...] += jnp.sum(total * weights[...].astype(F32), axis=-1, keepdims=True)
    total = total.astype(BF16)
    for r in range(rs):
        for j in range(zs):
            for t in range(nb // wp):
                at = j * nb + t * wp
                out[r, j, t * kb : (t + 1) * kb, :] = total[r * kb : (r + 1) * kb, at : at + wp]
    if not last:
        return

    @pl.when(step == pl.num_programs(0) - 1)
    def _():
        rs, zs, tall, wp = little_send.shape
        size = 128
        eye = lax.broadcasted_iota(jnp.int32, (size, size), 0) == lax.broadcasted_iota(
            jnp.int32, (size, size), 1
        )
        column = [first[i : i + size, :] for i in range(0, first.shape[0], size)]
        column = [jnp.sum(jnp.where(eye, part, 0.0), axis=0, keepdims=True) for part in column]
        lines = [gsmall[0:1, :], gsmall[1:2, :], jnp.concatenate(column, axis=1) / gain[...]]
        each = gain.shape[1] // (rs * zs * 2)

        def line_of(r, c):
            at = (r * zs * 2 + c) * each
            parts = [line[:, at : at + each] for line in lines]
            parts.append(jnp.zeros((1, wp - 3 * each), F32))
            return jnp.broadcast_to(jnp.concatenate(parts, axis=1), (tall, wp)).astype(BF16)

        for r in range(rs):
            for z in range(zs):
                pair = line_of(r, 2 * z), line_of(r, 2 * z + 1)
                split_out(bit[0], *pair, little_keep, little_send, (r, z))


def qkv_weight_grad(name, bit, x, y, w, shape, wp, count, small=(), deps=()):
    depth, rows = x.shape
    rs, cs, kb, nb = shape
    zs = cs // 2
    many = zs // count
    tall = kb * nb // wp
    step = 2 * many * nb
    out = pl.BlockSpec((rs, many, tall, wp), lambda j, _: (0, j, 0, 0))
    little = (rs, zs, 16, wp)
    grad = shaped((rs, zs, tall, wp), BF16)
    buffers = [pltpu.VMEM((rows, step // 2), BF16), pltpu.VMEM((depth, step // 2), BF16)]
    column = pltpu.VMEM((depth, 1), F32)
    if nb % 128 == 0:
        fetched = many

        def cut(tall, k):
            def place_of(j, bit):
                return 0, 2 * (many * j + k) + (bit[0] if small else 1 - bit[0])

            return pl.BlockSpec((tall, nb), place_of)

    else:
        fetched = 1

        def cut(tall, _):
            return pl.BlockSpec((tall, step), lambda j, _: (0, j))

    return call(
        functools.partial(qkv_grad_body, kb, nb, bool(small), fetched),
        name,
        (count,),
        [once(x.shape)]
        + [cut(rows, k) for k in range(fetched)]
        + [cut(depth, k) for k in range(fetched)]
        + [whole(each.shape) for each in small],
        [out, whole(little), whole(little)] if small else [out, whole((depth, 1))],
        [grad] + ([shaped(little, BF16)] * 2 if small else [shaped((depth, 1), F32)]),
        ([column] if small else []) + buffers,
        prefetch=1,
        flops=rows * depth * cs * nb,
        nbytes=x.size + y.size + 2 * w.size,
        deps=deps,
    )(bit, x, *[y] * fetched, *[w] * fetched, *small)


def feed_back_body(
    kb, ub, bit, grows, w, slope, hidden, gate, x_turned, w_up,
    natural, dots, send, keep, total,
):
    rs, _, tall, wp = w.shape
    pieces_up = kb // wp
    step = pl.program_id(0)
    lay_cr(w, natural, kb)

    @pl.when(step == 0)
    def _():
        dots[...] = jnp.zeros_like(dots)
        total[...] = jnp.zeros_like(total)

    def half(h, carry):
        at = slice(h * kb, (h + 1) * kb)
        back = mul(grows[...], natural[at, :], NT)
        gpre = (back * gate[...] * slope[:, at].astype(F32)).astype(BF16)
        product = back * hidden[:, at].astype(F32)
        summed = product[:, :128]
        for n in range(1, kb // 128):
            summed = summed + product[:, n * 128 : (n + 1) * 128]
        dots[...] += summed
        part = mul(x_turned[...], gpre).astype(BF16)

        def put(target):
            for r in range(rs):
                for t in range(pieces_up):
                    value = part[r * ub : (r + 1) * ub, t * wp : (t + 1) * wp]
                    target[r, 0, t * ub : (t + 1) * ub, :] = value

        @pl.when(bit[0] == h)
        def _():
            put(keep)

        @pl.when(bit[0] != h)
        def _():
            put(send)

        total[...] += mul(gpre, w_up[:, at], NT)
        return carry

    half(0, 0)
    half(1, 0)


def feed_back(bit, grows, w, slope, hidden, gate, x_turned, w_up, kb, ub, deps=()):
    rows, width = grows.shape
    rs, cs, tall, wp = w.shape
    zs = cs // 2
    deep = hidden.shape[1]
    fb = 2 * kb
    cut = pl.BlockSpec((rows, fb), lambda j, _: (0, j))
    half = (rs, zs, ub * kb // wp, wp)
    grad = pl.BlockSpec((rs, 1) + half[2:], lambda j, _: (0, j, 0, 0))
    return call(
        functools.partial(feed_back_body, kb, ub),
        "feed_back",
        (zs,),
        [once(grows.shape), pl.BlockSpec((rs, 2, tall, wp), lambda j, _: (0, j, 0, 0)), cut, cut]
        + [once(gate.shape), once(x_turned.shape), pl.BlockSpec((width, fb), lambda j, _: (0, j))],
        [
            pl.BlockSpec((fb, width), lambda j, _: (j, 0)),
            whole((rows, 128)),
            grad,
            grad,
            whole((rows, width)),
        ],
        [shaped((deep, width), BF16), shaped((rows, 128), F32)]
        + [shaped(half, BF16)] * 2
        + [shaped((rows, width), F32)],
        prefetch=1,
        flops=6 * rows * width * deep,
        nbytes=2 * (3 * width * deep + 2 * rows * deep + 4 * rows * width),
        deps=deps,
    )(bit, grows, w, slope, hidden, gate, x_turned, w_up)


def norm_back(grad, v, inverse, gain):
    scaled = grad * gain
    summed = jnp.sum(scaled * v, axis=-1, keepdims=True)
    return inverse * scaled - v * (inverse * inverse * inverse * summed / v.shape[-1])


def context_back_body(
    kb, nb, bit, total, attn, picked, grows, gate, dots, context, gain, w,
    gmid, gcontext, logit, gsmall, send, keep, gattn, gout,
):
    step = pl.program_id(0)

    @pl.when(step == 0)
    def _():
        gsmall[...] = jnp.zeros_like(gsmall)
        gout[...] = jnp.zeros_like(gout)

    chunk = 128

    def rows_back(i, carry):
        at = pl.ds(pl.multiple_of(i * chunk, chunk), chunk)
        grad = total[at, :]
        rows = picked[at, :].astype(F32)
        middle = rows + attn[at, :]
        inverse = lax.rsqrt(jnp.mean(middle * middle, axis=-1, keepdims=True) + EPSILON)
        gsmall[0:1, :] += jnp.sum(grad * middle * inverse, axis=0, keepdims=True)
        back = norm_back(grad, middle, inverse, gain[...])
        gmid[at, :] = back
        opened, dy = gate[at, :], grows[at, :].astype(F32)
        gattn[at, :] = (opened * dy + back).astype(BF16)
        opening = jnp.sum(dots[at, :], axis=-1, keepdims=True)
        opening += jnp.sum(dy * attn[at, :], axis=-1, keepdims=True)
        opening = opening * opened * (1.0 - opened)
        logit[at, :] = opening
        gsmall[1:2, :] += jnp.sum(opening * rows, axis=0, keepdims=True)
        return carry

    lax.fori_loop(0, total.shape[0] // chunk, rows_back, 0)
    gcontext[...] = mul(gattn[...], w[...], NT).astype(BF16)
    gout[...] += mul(context[...], gattn[...], TN)

    @pl.when(step == pl.num_programs(0) - 1)
    def _():
        grad_cr(bit[0], gout[...].astype(BF16), send, keep, kb, nb)


def context_back(
    bit, total, attn, picked, grows, gate, dots, context, gain, w, shape, wp, steps, deps=()
):
    rows, width = attn.shape
    rs, cs, kb, nb = shape
    half = (rs, cs // 2, kb * nb // wp, wp)
    size = rows // steps
    part = pl.BlockSpec((size, width), lambda j, _: (j, 0))
    thin = pl.BlockSpec((size, 1), lambda j, _: (j, 0))
    return call(
        functools.partial(context_back_body, kb, nb),
        "context_back",
        (steps,),
        [part] * 4
        + [thin, pl.BlockSpec((size, 128), lambda j, _: (j, 0)), part]
        + [once(gain.shape), once(w.shape)],
        [part, part, thin, whole((2, width)), whole(half), whole(half)],
        [
            shaped(attn.shape, F32),
            shaped(attn.shape, BF16),
            shaped(gate.shape, F32),
            shaped((2, width), F32),
            shaped(half, BF16),
            shaped(half, BF16),
        ],
        [pltpu.VMEM((size, width), BF16), pltpu.VMEM((width, width), F32)],
        prefetch=1,
        flops=4 * rows * width * width,
        nbytes=26 * rows * width + 6 * width * width,
        deps=deps,
    )(bit, total, attn, picked, grows, gate, dots, context, gain, w)


def attend_back_body(proj, gcontext, probs, out):
    routed = proj.shape[0]
    low, high = halves()
    tiles = [proj[:, i * 2 * HD : (i + 1) * 2 * HD] for i in range(3 * HEADS // 2)]
    grads, weights, grad_probs = [], [], []
    for pair in range(HEADS // 2):
        b, c = tiles[3 * pair + 1], tiles[3 * pair + 2]
        grad = gcontext[:, pair * 2 * HD : (pair + 1) * 2 * HD]
        grads += [grad * low, grad * high]
        for head in (2 * pair, 2 * pair + 1):
            weights.append(probs[0, head * routed : (head + 1) * routed, :])
        grad_probs += [mul(b, grads[-2], NT), mul(c, grads[-1], NT)]
    wide = [weight.astype(F32) for weight in weights]
    inner = [jnp.sum(g * w, axis=0, keepdims=True) for g, w in zip(grad_probs, wide)]
    backs = [(w * (g - i)).astype(BF16) for g, w, i in zip(grad_probs, wide, inner)]
    for pair in range(HEADS // 2):
        a, b, c = (turned(tile) for tile in tiles[3 * pair : 3 * pair + 3])
        (first, second), (low_grad, high_grad) = (
            each[2 * pair : 2 * pair + 2] for each in (backs, grads)
        )
        at = [slice((3 * pair + t) * 2 * HD, (3 * pair + t + 1) * 2 * HD) for t in range(3)]
        out[:, at[0]] = (mul(first, a * low, TN) + mul(first, a * high)).astype(BF16)
        out[:, at[1]] = (mul(weights[2 * pair], low_grad) + mul(second, c * high, TN)).astype(BF16)
        left = jnp.concatenate([second, weights[2 * pair + 1]], axis=1)
        right = jnp.concatenate([b * low, high_grad], axis=0)
        out[:, at[2]] = mul(left, right).astype(BF16)


def attend_back(projected, gcontext, probs, seqs, deps=()):
    rows, wide = projected.shape
    routed = rows // seqs
    return call(
        attend_back_body,
        "attend_back",
        (seqs,),
        [
            pl.BlockSpec((routed, wide), lambda s: (s, 0)),
            pl.BlockSpec((routed, wide // 3), lambda s: (s, 0)),
            pl.BlockSpec((1, HEADS * routed, routed), lambda s: (s, 0, 0)),
        ],
        pl.BlockSpec((routed, wide), lambda s: (s, 0)),
        shaped((rows, wide), BF16),
        flops=40 * rows * wide * routed,
        nbytes=16 * projected.size,
        deps=deps,
    )(projected, gcontext, probs)


def picked_back_body(
    places, gproj, w, logit, gain, router, picked, gmid, grows, base,
    out, total, picked_in, gmid_in, grows_in, fetched, arrived,
):
    j = pl.program_id(0)
    step = w.shape[0]
    loads = [
        pltpu.make_async_copy(source, target, fetched.at[i])
        for i, (source, target) in enumerate(
            ((picked, picked_in), (gmid, gmid_in), (grows, grows_in))
        )
    ]

    @pl.when(j == 0)
    def _():
        for load in loads:
            load.start()

    total[j] = mul(gproj[...], w[...], NT)

    @pl.when(j == pl.num_programs(0) - 1)
    def _():
        for load in loads:
            load.wait()
        chunk = 128
        count = total.shape[1] // chunk

        def compute(i):
            at = pl.ds(pl.multiple_of(i * chunk, chunk), chunk)
            grad = jnp.concatenate([total[n, at, :] for n in range(total.shape[0])], axis=1)
            rows = picked_in[at, :].astype(F32)
            inverse = lax.rsqrt(jnp.mean(rows * rows, axis=-1, keepdims=True) + EPSILON)
            back = norm_back(grad, rows, inverse, gain[...])
            gmid_in[at, :] = (
                gmid_in[at, :]
                + back
                + (logit[at, :] * router[...] + grows_in[at, :].astype(F32))
            )

        def copy(row):
            pltpu.make_async_copy(
                gmid_in.at[pl.ds(row, 1)], out.at[pl.ds(places[row], 1)], arrived
            ).start()

        def both(i, carry):
            for k in range(chunk):
                copy((i - 1) * chunk + k)
            compute(i)
            return carry

        def last(row, carry):
            copy(row)
            return carry

        compute(0)
        lax.fori_loop(1, count, both, 0)
        lax.fori_loop((count - 1) * chunk, count * chunk, last, 0, unroll=8)
        pltpu.make_async_copy(gmid_in, out.at[pl.ds(0, gmid_in.shape[0])], arrived).wait()


def picked_back(places, gproj, w, picked, gmid, logit, grows, gain, router, base, step, deps=()):
    rows, deep = gproj.shape
    width = picked.shape[1]
    return call(
        picked_back_body,
        "picked_back",
        (width // step,),
        [once(gproj.shape), pl.BlockSpec((step, deep), lambda j, _: (j, 0))]
        + [once(t.shape) for t in (logit, gain, router)]
        + [pl.BlockSpec(memory_space=pl.ANY)] * 4,
        pl.BlockSpec(memory_space=pl.ANY),
        shaped(base.shape, F32),
        [
            pltpu.VMEM((width // step, rows, step), F32),
            pltpu.VMEM((rows, width), BF16),
            pltpu.VMEM((rows, width), F32),
            pltpu.VMEM((rows, width), BF16),
            pltpu.SemaphoreType.DMA((3,)),
            pltpu.SemaphoreType.DMA,
        ],
        prefetch=1,
        flops=2 * rows * deep * width,
        nbytes=2 * (gproj.size + w.size) + 10 * picked.size,
        alias={9: 0},
        deps=deps,
    )(places, gproj, w, logit, gain, router, picked, gmid, grows, base)


def join_body(count, *refs):
    out, at = refs[-1], 0
    for keep, got in zip(refs[:count], refs[count : 2 * count]):
        tall = keep.shape[2]

        def add(z, carry):
            total = keep[0, z].astype(F32) + got[0, z].astype(F32)
            out[0, z, at : at + tall, :] = total.astype(BF16)
            return carry

        lax.fori_loop(0, keep.shape[1], add, 0)
        at += tall


def joined(keeps, gots, deps=()):
    rs, zs, _, wp = keeps[0].shape
    talls = [k.shape[2] for k in keeps]
    blocks = [pl.BlockSpec((1, zs, tall, wp), lambda r: (r, 0, 0, 0)) for tall in talls]
    tall = sum(talls)
    return call(
        functools.partial(join_body, len(keeps)),
        "join",
        (rs,),
        blocks * 2,
        pl.BlockSpec((1, zs, tall, wp), lambda r: (r, 0, 0, 0)),
        pltpu.HBM((rs, zs, tall, wp), BF16),
        flops=rs * zs * tall * wp,
        nbytes=6 * rs * zs * tall * wp,
        vmem=40,
        deps=deps,
    )(*[pltpu.with_memory_space_constraint(keep, pltpu.HBM) for keep in keeps], *gots)


def lower_body(hidden, w, attn, picked, gate, kept):
    branch = attn[...] + mul(hidden[...], w[...])
    kept[...] = (picked[...].astype(F32) + gate[...] * branch).astype(BF16)


def lowered(hidden, w, attn, picked, gate, step, deps=()):
    rows, deep = hidden.shape
    width = w.shape[1]
    cut = pl.BlockSpec((rows, step), lambda j: (0, j))
    return call(
        lower_body,
        "lower",
        (width // step,),
        [whole(hidden.shape), pl.BlockSpec((deep, step), lambda j: (0, j))]
        + [cut] * 2
        + [whole(gate.shape)],
        cut,
        shaped((rows, width), BF16),
        flops=2 * rows * deep * width,
        nbytes=2 * (hidden.size + w.size) + 8 * attn.size,
        deps=deps,
    )(hidden, w, attn, picked, gate)


def place_body(index, tok, kept, output):
    found = one_hot(index, tok.shape[0])
    hot = jnp.where(found, 1.0, 0.0)
    routed = jnp.sum(hot, axis=-1, keepdims=True) > 0.5
    output[...] = jnp.where(
        routed, mul(hot.astype(BF16), kept[...]), tok[...].astype(F32)
    ).astype(BF16)


def place(tokens, index, kept, deps=()):
    seqs, _, routed = index.shape
    length, width = tokens.shape[0] // seqs, tokens.shape[1]
    whole_seq = pl.BlockSpec((length, width), lambda s: (s, 0))
    return call(
        place_body,
        "place",
        (seqs,),
        [
            pl.BlockSpec((1, 1, routed), lambda s: (s, 0, 0)),
            whole_seq,
            pl.BlockSpec((routed, width), lambda s: (s, 0)),
        ],
        whole_seq,
        shaped(tokens.shape, BF16),
        flops=2 * seqs * routed * length * width,
        nbytes=4 * tokens.size,
        deps=deps,
    )(index, tokens, kept)


def pieces_body(qkv, out, up, down, small, first, second, third):
    def lay(target, at, block):
        kb, nb = block.shape
        wp = target.shape[1]
        for t in range(nb // wp):
            target[at + t * kb : at + (t + 1) * kb, :] = block[:, t * wp : (t + 1) * wp]

    kb, nb = qkv.shape
    wp = first.shape[1]
    size = kb // 2
    middle = kb * nb // wp // 2
    for t in range(2 * nb // wp):
        at = t * size + (16 if t * size >= middle else 0)
        value = qkv[t % 2 * size : (t % 2 + 1) * size, t // 2 * wp : (t // 2 + 1) * wp]
        first[at : at + size, :] = value
    first[middle : middle + 16, :] = small[...]
    first[2 * middle + 16 :, :] = jnp.zeros_like(small)
    lay(second, 0, up)
    lay(second, up.shape[0] * up.shape[1] // wp, out)
    lay(third, 0, down)


def pieces(qkv, out, up, down, small):
    wp = small.shape[1]
    talls = (qkv.size // wp + 32, (up.size + out.size) // wp, down.size // wp)
    return call(
        pieces_body,
        "pieces",
        (1,),
        [whole(w.shape) for w in (qkv, out, up, down, small)],
        [whole((tall, wp)) for tall in talls],
        [shaped((tall, wp), BF16) for tall in talls],
        nbytes=4 * sum(talls) * wp,
        vmem=60,
    )(qkv, out, up, down, small)


def gathered(flat, rs, cs):
    return lax.all_gather(flat, BOTH, axis=0, tiled=True).reshape(rs, cs, *flat.shape)


def shifted(value, part, shift, rs, cs):
    side = math.isqrt(rs)
    if part == "x":
        moves = [(r, r // side * side + (r + shift) % side) for r in range(rs)]
    elif part == "y":
        moves = [(r, (r + shift * side) % rs) for r in range(rs)]
    else:
        moves = [(c, (c + 2 * shift) % cs) for c in range(cs)]
    return lax.ppermute(value, "col" if part == "z" else "row", moves)


def permuted(flat, rs, cs, during):
    side, zs = math.isqrt(rs), cs // 2
    line = [flat] + [shifted(flat, "z", i, rs, cs) for i in range(1, zs)]
    line[0] = tied(flat, during[0])
    tall = flat.shape[0] // 2
    held = [jnp.stack([part[h * tall : (h + 1) * tall] for part in line])[None] for h in range(2)]
    for order in ("xy", "yx"):
        moved = [
            [shifted(h, part, i, rs, cs) for i in range(1, side)] for h, part in zip(held, order)
        ]
        if order == "xy":
            done, result = during[1](held[0])
        else:
            done, result = during[2](held[0], result)
        held[0] = tied(held[0], done)
        held = [jnp.concatenate([h] + m) for h, m in zip(held, moved)]
    pairs = [(c, c ^ 1) for c in range(cs)]
    return held + [lax.ppermute(h, "col", pairs) for h in held], result


def spots_of(rs, cs):
    side, zs = math.isqrt(rs), cs // 2
    row, column = lax.axis_index("row"), lax.axis_index("col")
    r, z = jnp.arange(rs), jnp.arange(zs)
    y, x = (row // side - r // side) % side, (row - r) % side
    table = jnp.zeros((4, max(rs, zs)), jnp.int32)
    table = table.at[0, :rs].set(y * side + x).at[1, :rs].set(x * side + y)
    return table.at[2, :].set(column % 2).at[3, :zs].set((column // 2 - z) % zs)


def local(
    tokens,
    router_weight,
    norm_first,
    qkv_weight,
    out_weight,
    norm_second,
    up_weight,
    down_weight,
    route_index,
    out_cotangent,
    rs,
    cs,
):
    seqs, routed = route_index.shape
    width = tokens.shape[1]
    index = route_index.reshape(seqs, 1, routed)
    column = lax.axis_index("col")
    core, depth = column % 2, column // 2
    zs = cs // 2
    bit = core.astype(jnp.int32).reshape(1)
    pairs = [(c, c ^ 1) for c in range(cs)]
    blocks = [w.shape for w in (qkv_weight, out_weight, up_weight, down_weight)]
    shape_qkv, shape_out, shape_up, shape_down = ((rs, cs) + b for b in blocks)
    wp = math.gcd(128, *(b[1] for b in blocks))
    tall_qkv, tall_out, tall_up, tall_down = (b[0] * b[1] // wp for b in blocks)

    spots = spots_of(rs, cs)
    small = jnp.concatenate([router_weight, norm_first, norm_second])
    small = jnp.pad(small.reshape(1, -1), ((0, 15), (0, wp - small.shape[0])))
    flat, next_flat, down_flat = pieces(qkv_weight, out_weight, up_weight, down_weight, small)

    def pick_first(dep):
        result = pick("pick_first", out_cotangent, index, True, 0, seqs // 3, deps=(dep,))
        return result[0], result

    def pick_rest(dep, begun):
        result = pick("pick_rest", out_cotangent, index, True, seqs // 3, None, begun, deps=(dep,))
        return result[0], result

    picked = pick("pick", tokens, index, False)
    parts, (grows, base) = permuted(flat, rs, cs, (picked, pick_first, pick_rest))
    next_parts = gathered(next_flat, rs, cs)
    down_parts = gathered(down_flat, rs, cs)

    def exchanged(send):
        return lax.ppermute(send, "col", pairs)

    def by_row(keep):
        r, z, tall, _ = keep.shape
        mine = lax.psum_scatter(
            keep.reshape(r * z * tall, wp), "row", scatter_dimension=0, tiled=True
        )
        return mine.reshape(z, tall, wp)

    def depth_parts(mine):
        return [
            lax.dynamic_index_in_dim(mine, (depth + shift) % zs, 0, keepdims=False)
            for shift in range(zs)
        ]

    def depth_sum(parts, *deps):
        total = (tied(parts[0], *deps) if deps else parts[0]).astype(F32)
        for shift in range(1, zs):
            total = total + shifted(parts[shift], "z", shift, rs, cs).astype(F32)
        return total

    def block(total, shape):
        kb, nb = shape[2:]
        return jnp.concatenate([total[i : i + kb] for i in range(0, kb * nb // wp, kb)], axis=1)

    projected, w_qkv, turned_normed, gmlp, gate, small = project(
        spots, picked, grows, parts, blocks[0][0], blocks[0][1] // wp
    )
    router, first_gain, second_gain = small[0:1], small[1:2], small[2:3]
    context, probs = attend(projected, seqs)
    attn, normed_mid, mid_turned, w_out = mix(
        context, next_parts, tall_up // tall_out, tall_out, blocks[1][0], picked, second_gain, 3
    )
    hidden, slope, w_up, down_send, down_keep = raised(
        bit, normed_mid, gmlp, next_parts, 0, tall_up, blocks[2][0], shape_down
    )
    down_keep = joined([down_keep], [exchanged(down_send)])
    down_rows = by_row(down_keep)

    w_down, dots, up_send, up_keep, gnormed = feed_back(
        bit, grows, down_parts, slope, hidden, gate, mid_turned, w_up,
        blocks[3][0], blocks[2][0], deps=(down_keep,),
    )
    up_keep = joined([up_keep], [exchanged(up_send)])
    up_rows = by_row(up_keep)
    gmid, gcontext, logit, gsmall, out_send, out_keep = context_back(
        bit, gnormed, attn, picked, grows, gate, dots, context, second_gain, w_out, shape_out,
        wp, 3, deps=(up_keep,),
    )

    gproj = attend_back(projected, gcontext, probs, seqs)
    qkv_send, gfirst = qkv_weight_grad(
        "qkv_send", bit, turned_normed, gproj, w_qkv, shape_qkv, wp, 2
    )
    qkv_keep, little_send, little_keep = qkv_weight_grad(
        "qkv_keep", bit, turned_normed, gproj, w_qkv, shape_qkv, wp, 2,
        (gsmall, first_gain, gfirst), deps=(qkv_send,),
    )
    qkv_keep = joined(
        [qkv_keep, out_keep, little_keep],
        [exchanged(qkv_send), exchanged(out_send), exchanged(little_send)],
    )
    qkv_rows = by_row(qkv_keep)

    feed_parts = depth_parts(jnp.concatenate([down_rows, up_rows], axis=1))
    starts = jnp.arange(seqs, dtype=jnp.int32) * (tokens.shape[0] // seqs)
    places = (route_index + starts[:, None]).reshape(-1)
    input_grad = picked_back(
        places, gproj, w_qkv, picked, gmid, logit, grows, first_gain, router, base, 256,
        deps=(qkv_keep, *feed_parts),
    )
    kept = lowered(hidden, w_down, attn, picked, gate, 256, deps=(input_grad,))
    feed_total = depth_sum(feed_parts, kept)
    qkv_parts = depth_parts(qkv_rows)
    output = place(tokens, index, kept, deps=(*qkv_parts, feed_total))
    qkv_total = depth_sum(qkv_parts, output)
    down_grad = block(feed_total[:tall_down], shape_down)
    up_grad = block(feed_total[tall_down:], shape_up)
    out_grad = block(qkv_total[tall_qkv : tall_qkv + tall_out], shape_out)
    qkv_grad = block(qkv_total[:tall_qkv], shape_qkv)
    sums = qkv_total[tall_qkv + tall_out, : 3 * width // (rs * cs)].reshape(3, -1)
    return (
        output,
        input_grad,
        sums[1],
        sums[2],
        qkv_grad,
        out_grad,
        sums[0],
        up_grad,
        down_grad,
    )


def solution(mesh):
    both, by_row, by_col = P(BOTH), P("row", "col"), P("col", "row")
    tall = P(BOTH, None)
    return jax.shard_map(
        functools.partial(local, rs=mesh.shape["row"], cs=mesh.shape["col"]),
        mesh=mesh,
        in_specs=(tall, both, both, by_row, by_col, both, by_row, by_col, tall, tall),
        out_specs=(tall, tall, both, both, by_row, by_col, both, by_row, by_col),
        check_vma=False,
    )
```

```python
import functools
import math

import jax
import jax.numpy as jnp
from jax import lax
from jax.experimental import pallas as pl
from jax.experimental.pallas import tpu as pltpu
from jax.sharding import PartitionSpec as P

HEADS = 16
HD = 64
EPSILON = 1e-06
F32 = jnp.float32
BF16 = jnp.bfloat16
BOTH = ("row", "col")
SLOW = 1

NN = (((1,), (0,)), ((), ()))
NT = (((1,), (1,)), ((), ()))
TN = (((0,), (0,)), ((), ()))


def mul(a, b, dims=NN):
    return lax.dot_general(a, b, dims, preferred_element_type=F32)


def call(
    body, name, grid, ins, outs, shapes, scratch=(), prefetch=0, flops=0, nbytes=0, deps=(), alias=None, vmem=56
):
    count = prefetch + len(ins)

    def run(*refs):
        body(*refs[:count], *refs[count + len(deps) :])

    made = pl.pallas_call(
        run,
        name=name,
        grid_spec=pltpu.PrefetchScalarGridSpec(
            num_scalar_prefetch=prefetch,
            grid=grid,
            in_specs=ins + [pl.BlockSpec(memory_space=pl.ANY)] * len(deps),
            out_specs=outs,
            scratch_shapes=list(scratch),
        ),
        out_shape=shapes,
        input_output_aliases=alias or {},
        compiler_params=pltpu.CompilerParams(
            dimension_semantics=("arbitrary",) * len(grid),
            vmem_limit_bytes=vmem * 2**20,
        ),
        cost_estimate=pl.CostEstimate(
            flops=flops // SLOW, transcendentals=0, bytes_accessed=nbytes // SLOW
        ),
    )
    return lambda *args: made(*args, *deps)


def tied(value, *deps):
    return call(
        lambda given, out: None,
        "tied",
        (1,),
        [pl.BlockSpec(memory_space=pl.ANY)],
        pl.BlockSpec(memory_space=pl.ANY),
        shaped(value.shape, value.dtype),
        deps=deps,
        alias={0: 0},
        vmem=60,
    )(value)


def whole(shape):
    return pl.BlockSpec(shape, lambda *_: (0,) * len(shape))


def once(shape):
    return pl.BlockSpec(shape, lambda *_: (0,) * len(shape), pipeline_mode=pl.Buffered(1))


def shaped(shape, dtype):
    return jax.ShapeDtypeStruct(shape, dtype)


def one_hot(index_ref, length):
    places = lax.broadcasted_iota(jnp.int32, (length, index_ref.shape[-1]), 0)
    return places == index_ref[0]


def pick_cot_body(index, cot, grows, base):
    hot = jnp.where(one_hot(index, cot.shape[0]), 1.0, 0.0).astype(BF16)
    grows[...] = mul(hot, cot[...], TN).astype(BF16)
    base[...] = cot[...].astype(F32)


def pick_body(index, tok, picked):
    hot = jnp.where(one_hot(index, tok.shape[0]), 1.0, 0.0).astype(BF16)
    picked[...] = mul(hot, tok[...], TN).astype(BF16)


def pick(name, source, index, with_copy, start=0, stop=None, begun=(), deps=()):
    seqs, _, routed = index.shape
    length, width = source.shape[0] // seqs, source.shape[1]
    whole_seq = pl.BlockSpec((length, width), lambda s: (s + start, 0))
    part = pl.BlockSpec((routed, width), lambda s: (s + start, 0))
    rows = shaped((seqs * routed, width), BF16)
    return call(
        functools.partial(begun_body, pick_cot_body if with_copy else pick_body, len(begun)),
        name,
        ((stop or seqs) - start,),
        [pl.BlockSpec((1, 1, routed), lambda s: (s + start, 0, 0)), whole_seq]
        + [pl.BlockSpec(memory_space=pl.ANY)] * len(begun),
        [part, whole_seq] if with_copy else part,
        [rows, shaped(source.shape, F32)] if with_copy else rows,
        flops=2 * seqs * routed * length * width,
        nbytes=6 * source.size,
        deps=deps,
        alias={2 + i: i for i in range(len(begun))},
    )(index, source, *begun)


def begun_body(body, count, index, source, *refs):
    body(index, source, *refs[count:])


def lay_rc(w, buf, kb):
    rs, cs, tall, wp = w.shape
    pieces = tall // kb
    for r in range(rs):
        for c in range(cs):
            for t in range(pieces):
                at = (c * pieces + t) * wp
                buf[r * kb : (r + 1) * kb, at : at + wp] = w[r, c, t * kb : (t + 1) * kb, :]


def lay_cr(w, buf, kb):
    rs, cs, tall, wp = w.shape
    pieces = tall // kb
    for r in range(rs):
        for c in range(cs):
            for t in range(pieces):
                at = (r * pieces + t) * wp
                buf[c * kb : (c + 1) * kb, at : at + wp] = w[r, c, t * kb : (t + 1) * kb, :]


def lay_turned(spots, own, other, place, rs, zs, looped=False):
    bit = spots[2, 0]
    for core in range(2):

        def lay(r, carry):
            for z in range(zs):
                place(r, z, core, own)
                place(r, z, 1 - core, other)
            return carry

        @pl.when(bit == core)
        def _():
            if looped:
                lax.fori_loop(0, rs, lay, 0)
            else:
                for r in range(rs):
                    lay(r, 0)


def project_body(
    kb, wp, count, spots, picked, grows, own_a, own_b, other_a, other_b, own_s, other_s,
    out, natural, normed_turned, gmlp, gate, small, normed,
):
    rs, zs = own_s.shape[:2]
    tall = kb * count // 2
    rows, width = picked.shape
    each = width // (rs * zs * 2)

    def place_small(r, z, core, source):
        at = (r * zs * 2 + 2 * z + core) * each
        line = source[spots[0, r], spots[3, z], 0:16, :].astype(F32)
        for k in range(3):
            small[k : k + 1, at : at + each] = line[0:1, k * each : (k + 1) * each]

    @pl.when(pl.program_id(0) == 0)
    def _():
        lay_turned(spots, own_s, other_s, place_small, rs, zs)
        chunk = 128

        def prepare(i, carry):
            at = pl.ds(pl.multiple_of(i * chunk, chunk), chunk)
            value = picked[at, :].astype(F32)
            opened = jax.nn.sigmoid(jnp.sum(value * small[0:1, :], axis=-1, keepdims=True))
            inverse = lax.rsqrt(jnp.mean(value * value, axis=-1, keepdims=True) + EPSILON)
            scaled = (value * inverse * small[1:2, :]).astype(BF16)
            normed[at, :] = scaled
            normed_turned[:, at] = scaled.T
            gmlp[at, :] = (grows[at, :].astype(F32) * opened).astype(BF16)
            gate[at, :] = opened
            return carry

        lax.fori_loop(0, rows // chunk, prepare, 0)

    def place(r, z, core, halves_of):
        size = kb // 2
        for t in range(2 * count):
            half, at = divmod(t * size, tall)
            value = halves_of[half][spots[half, r], 0, at : at + size, :]
            lane = (core * count + t // 2) * wp
            down = pl.multiple_of(r * kb + t % 2 * size, size)
            natural[pl.ds(down, size), lane : lane + wp] = value

    lay_turned(spots, (own_a, own_b), (other_a, other_b), place, rs, 1, looped=True)
    out[...] = mul(normed[...], natural[...]).astype(BF16)


def project(spots, picked, grows, parts, kb, count):
    rows, depth = picked.shape
    rs, zs, tall, wp = parts[0].shape
    step = 2 * count * wp
    piece = pl.BlockSpec((rs, 1, tall, wp), lambda j, spots: (0, spots[3, j], 0, 0))
    last = pl.BlockSpec((rs, zs, 16, wp), lambda j, _: (0, 0, tall // 16 - 1, 0))
    return call(
        functools.partial(project_body, kb, wp, count),
        "project",
        (zs,),
        [whole(picked.shape)] * 2 + [piece] * 4 + [last] * 2,
        [
            pl.BlockSpec((rows, step), lambda j, _: (0, j)),
            pl.BlockSpec((depth, step), lambda j, _: (0, j)),
            whole((depth, rows)),
            whole(picked.shape),
            whole((rows, 1)),
            whole((3, depth)),
        ],
        [
            shaped((rows, zs * step), BF16),
            shaped((depth, zs * step), BF16),
            shaped((depth, rows), BF16),
            shaped(picked.shape, BF16),
            shaped((rows, 1), F32),
            shaped((3, depth), F32),
        ],
        [pltpu.VMEM((rows, depth), BF16)],
        prefetch=1,
        flops=2 * rows * depth * zs * step,
        nbytes=2 * (4 * picked.size + 2 * depth * zs * step + rows * zs * step),
    )(spots, picked, grows, *parts, parts[0], parts[2])


def halves():
    lane = lax.broadcasted_iota(jnp.int32, (1, 2 * HD), 1)
    low = jnp.where(lane < HD, 1.0, 0.0).astype(BF16)
    high = jnp.where(lane < HD, 0.0, 1.0).astype(BF16)
    return low, high


def turned(x):
    return jnp.concatenate([x[:, HD:], x[:, :HD]], axis=1) * jnp.asarray(HD**-0.5, BF16)


def causal_of(routed):
    return lax.broadcasted_iota(jnp.int32, (routed, routed), 0) <= lax.broadcasted_iota(
        jnp.int32, (routed, routed), 1
    )


def attend_body(proj, context, probs, context_turned):
    routed = proj.shape[0]
    low, high = halves()
    causal = causal_of(routed)
    tiles = [proj[:, i * 2 * HD : (i + 1) * 2 * HD] for i in range(3 * HEADS // 2)]
    scores = []
    for a, b, c in zip(tiles[::3], tiles[1::3], tiles[2::3]):
        scores.append(mul(turned(a) * low, a, NT))
        scores.append(mul(turned(c) * high, b, NT))
    scores = [jnp.where(causal, score, -1e30) for score in scores]
    highest = [jnp.max(score, axis=0, keepdims=True) for score in scores]
    expanded = [jnp.exp(score - top) for score, top in zip(scores, highest)]
    inverse = [1.0 / jnp.sum(e, axis=0, keepdims=True) for e in expanded]
    weights = [(e * i).astype(BF16) for e, i in zip(expanded, inverse)]
    for pair in range(HEADS // 2):
        b, c = tiles[3 * pair + 1], tiles[3 * pair + 2]
        both = jnp.concatenate(weights[2 * pair : 2 * pair + 2], axis=0)
        probs[0, 2 * pair * routed : 2 * (pair + 1) * routed, :] = both
        mixed = mul(both, jnp.concatenate([b * low, c * high], axis=0), TN)
        mixed = mixed.astype(BF16)
        context[:, pair * 2 * HD : (pair + 1) * 2 * HD] = mixed
        context_turned[pair * 2 * HD : (pair + 1) * 2 * HD, :] = mixed.T


def attend(projected, seqs):
    rows, wide = projected.shape
    routed = rows // seqs
    width = wide // 3
    return call(
        attend_body,
        "attend",
        (seqs,),
        [pl.BlockSpec((routed, wide), lambda s: (s, 0))],
        [
            pl.BlockSpec((routed, width), lambda s: (s, 0)),
            pl.BlockSpec((1, HEADS * routed, routed), lambda s: (s, 0, 0)),
            pl.BlockSpec((width, routed), lambda s: (0, s)),
        ],
        [
            shaped((rows, width), BF16),
            shaped((seqs, HEADS * routed, routed), BF16),
            shaped((width, rows), BF16),
        ],
        flops=20 * rows * wide * routed,
        nbytes=8 * projected.size,
    )(projected)


def mix_body(kb, context, w, picked, gain, attn, normed, turned_out, natural):
    @pl.when(pl.program_id(0) == 0)
    def _():
        lay_cr(w, natural, kb)

    out = mul(context[...], natural[...])
    attn[...] = out
    middle = picked[...].astype(F32) + out
    inverse = lax.rsqrt(jnp.mean(middle * middle, axis=-1, keepdims=True) + EPSILON)
    value = (middle * inverse * gain[...]).astype(BF16)
    normed[...] = value
    turned_out[...] = value.T


def mix(context, w, at, tall, kb, picked, gain, steps):
    rows, width = context.shape
    rs, cs, _, wp = w.shape
    part = pl.BlockSpec((rows // steps, width), lambda s: (s, 0))
    return call(
        functools.partial(mix_body, kb),
        "mix",
        (steps,),
        [part, pl.BlockSpec((rs, cs, tall, wp), lambda s: (0, 0, at, 0)), part, whole(gain.shape)],
        [part, part, pl.BlockSpec((width, rows // steps), lambda s: (0, s)), whole((width, width))],
        [
            shaped((rows, width), F32),
            shaped((rows, width), BF16),
            shaped((width, rows), BF16),
            shaped((width, width), BF16),
        ],
        flops=2 * rows * width * width,
        nbytes=14 * rows * width,
    )(context, w, picked, gain)


GELU_A = 0.7978845608028654
GELU_B = 0.044715


def raise_body(kb, bit, x, gmlp, w, hidden, slope, natural, send, keep):
    lay_rc(w, natural, kb)
    rs, _, tall, wp = send.shape
    fb = hidden.shape[1] // 2

    def half_of(h, carry):
        across = pl.ds(pl.multiple_of(h * fb, fb), fb)
        pre = mul(x[...], natural[:, across])
        square = pre * pre
        half = 0.5 + 0.5 * jnp.tanh(pre * (GELU_A + (GELU_A * GELU_B) * square))
        value = pre * half
        hidden[:, across] = value.astype(BF16)
        slope[:, across] = (
            half + value * (1.0 - half) * (2 * GELU_A + (6 * GELU_A * GELU_B) * square)
        ).astype(BF16)
        total = mul(hidden[:, across], gmlp[...], TN).astype(BF16)
        many = tall // fb

        def put(target):
            for r in range(rs):
                for t in range(many):
                    lane = (r * many + t) * wp
                    target[r, 0, t * fb : (t + 1) * fb, :] = total[:, lane : lane + wp]

        @pl.when(bit[0] == h)
        def _():
            put(keep)

        @pl.when(bit[0] != h)
        def _():
            put(send)

        return carry

    lax.fori_loop(0, 2, half_of, 0)


def raised(bit, x, gmlp, w, at, tall, kb, shape):
    rows, depth = x.shape
    rs, cs, _, wp = w.shape
    fb = (tall // kb) * wp
    zs = cs // 2
    out = pl.BlockSpec((rows, 2 * fb), lambda j, _: (0, j))
    half = (rs, zs, shape[2] * shape[3] // wp, wp)
    grad = pl.BlockSpec((rs, 1) + half[2:], lambda j, _: (0, j, 0, 0))
    return call(
        functools.partial(raise_body, kb),
        "raise",
        (zs,),
        [once(x.shape), once(gmlp.shape)]
        + [pl.BlockSpec((rs, 2, tall, wp), lambda j, _: (0, j, at, 0))],
        [out, out, pl.BlockSpec((depth, 2 * fb), lambda j, _: (0, j)), grad, grad],
        [shaped((rows, cs * fb), BF16)] * 2
        + [shaped((depth, cs * fb), BF16)]
        + [shaped(half, BF16)] * 2,
        prefetch=1,
        flops=5 * rows * depth * cs * fb,
        nbytes=2 * (x.size + 3 * depth * cs * fb + 2 * rows * cs * fb),
    )(bit, x, gmlp, w)


def split_out(bit, first, second, keep, send, at):
    @pl.when(bit == 0)
    def _():
        keep[at] = first
        send[at] = second

    @pl.when(bit != 0)
    def _():
        keep[at] = second
        send[at] = first


def grad_cr(bit, total, send, keep, kb, nb):
    rs, zs, _, wp = send.shape
    for r in range(rs):
        for j in range(zs):
            for t in range(nb // wp):
                across = slice(r * nb + t * wp, r * nb + (t + 1) * wp)
                where = (r, j, slice(t * kb, (t + 1) * kb))
                at = 2 * j * kb
                split_out(
                    bit, total[at : at + kb, across], total[at + kb : at + 2 * kb, across], keep, send, where
                )


def qkv_grad_body(kb, nb, last, many, bit, x, *refs):
    y, w, refs = refs[:many], refs[many : 2 * many], refs[2 * many :]
    if last:
        gsmall, gain, before, out, little_send, little_keep, first, columns, weights = refs
    else:
        out, first, columns, weights = refs
    step = pl.program_id(0)
    rs, zs, _, wp = out.shape
    side_here = bit[0] if last else 1 - bit[0]
    if many > 1:
        for j in range(zs):
            columns[:, j * nb : (j + 1) * nb] = y[j][...]
            weights[:, j * nb : (j + 1) * nb] = w[j][...]
    else:
        for side in range(2):

            @pl.when(side_here == side)
            def _():
                for j in range(zs):
                    source = slice((2 * j + side) * nb, (2 * j + side + 1) * nb)
                    target = slice(j * nb, (j + 1) * nb)
                    columns[:, target] = y[0][:, source]
                    weights[:, target] = w[0][:, source]

    @pl.when(step == 0)
    def _():
        first[...] = before[...] if last else jnp.zeros_like(first)

    total = mul(x[...], columns[...])
    first[...] += jnp.sum(total * weights[...].astype(F32), axis=-1, keepdims=True)
    total = total.astype(BF16)
    for r in range(rs):
        for j in range(zs):
            for t in range(nb // wp):
                at = j * nb + t * wp
                out[r, j, t * kb : (t + 1) * kb, :] = total[r * kb : (r + 1) * kb, at : at + wp]
    if not last:
        return

    @pl.when(step == pl.num_programs(0) - 1)
    def _():
        rs, zs, tall, wp = little_send.shape
        size = 128
        eye = lax.broadcasted_iota(jnp.int32, (size, size), 0) == lax.broadcasted_iota(
            jnp.int32, (size, size), 1
        )
        column = [first[i : i + size, :] for i in range(0, first.shape[0], size)]
        column = [jnp.sum(jnp.where(eye, part, 0.0), axis=0, keepdims=True) for part in column]
        lines = [gsmall[0:1, :], gsmall[1:2, :], jnp.concatenate(column, axis=1) / gain[...]]
        each = gain.shape[1] // (rs * zs * 2)

        def line_of(r, c):
            at = (r * zs * 2 + c) * each
            parts = [line[:, at : at + each] for line in lines]
            parts.append(jnp.zeros((1, wp - 3 * each), F32))
            return jnp.broadcast_to(jnp.concatenate(parts, axis=1), (tall, wp)).astype(BF16)

        for r in range(rs):
            for z in range(zs):
                pair = line_of(r, 2 * z), line_of(r, 2 * z + 1)
                split_out(bit[0], *pair, little_keep, little_send, (r, z))


def qkv_weight_grad(name, bit, x, y, w, shape, wp, count, small=(), deps=()):
    depth, rows = x.shape
    rs, cs, kb, nb = shape
    zs = cs // 2
    many = zs // count
    tall = kb * nb // wp
    step = 2 * many * nb
    out = pl.BlockSpec((rs, many, tall, wp), lambda j, _: (0, j, 0, 0))
    little = (rs, zs, 16, wp)
    grad = shaped((rs, zs, tall, wp), BF16)
    buffers = [pltpu.VMEM((rows, step // 2), BF16), pltpu.VMEM((depth, step // 2), BF16)]
    column = pltpu.VMEM((depth, 1), F32)
    if nb % 128 == 0:
        fetched = many

        def cut(tall, k):
            def place_of(j, bit):
                return 0, 2 * (many * j + k) + (bit[0] if small else 1 - bit[0])

            return pl.BlockSpec((tall, nb), place_of)

    else:
        fetched = 1

        def cut(tall, _):
            return pl.BlockSpec((tall, step), lambda j, _: (0, j))

    return call(
        functools.partial(qkv_grad_body, kb, nb, bool(small), fetched),
        name,
        (count,),
        [once(x.shape)]
        + [cut(rows, k) for k in range(fetched)]
        + [cut(depth, k) for k in range(fetched)]
        + [whole(each.shape) for each in small],
        [out, whole(little), whole(little)] if small else [out, whole((depth, 1))],
        [grad] + ([shaped(little, BF16)] * 2 if small else [shaped((depth, 1), F32)]),
        ([column] if small else []) + buffers,
        prefetch=1,
        flops=rows * depth * cs * nb,
        nbytes=x.size + y.size + 2 * w.size,
        deps=deps,
    )(bit, x, *[y] * fetched, *[w] * fetched, *small)


def feed_back_body(
    kb, ub, bit, grows, w, slope, hidden, gate, x_turned, w_up,
    natural, dots, send, keep, total,
):
    rs, _, tall, wp = w.shape
    pieces_up = kb // wp
    step = pl.program_id(0)
    lay_cr(w, natural, kb)

    @pl.when(step == 0)
    def _():
        dots[...] = jnp.zeros_like(dots)
        total[...] = jnp.zeros_like(total)

    def half(h, carry):
        at = slice(h * kb, (h + 1) * kb)
        back = mul(grows[...], natural[at, :], NT)
        gpre = (back * gate[...] * slope[:, at].astype(F32)).astype(BF16)
        product = back * hidden[:, at].astype(F32)
        summed = product[:, :128]
        for n in range(1, kb // 128):
            summed = summed + product[:, n * 128 : (n + 1) * 128]
        dots[...] += summed
        part = mul(x_turned[...], gpre).astype(BF16)

        def put(target):
            for r in range(rs):
                for t in range(pieces_up):
                    value = part[r * ub : (r + 1) * ub, t * wp : (t + 1) * wp]
                    target[r, 0, t * ub : (t + 1) * ub, :] = value

        @pl.when(bit[0] == h)
        def _():
            put(keep)

        @pl.when(bit[0] != h)
        def _():
            put(send)

        total[...] += mul(gpre, w_up[:, at], NT)
        return carry

    half(0, 0)
    half(1, 0)


def feed_back(bit, grows, w, slope, hidden, gate, x_turned, w_up, kb, ub, deps=()):
    rows, width = grows.shape
    rs, cs, tall, wp = w.shape
    zs = cs // 2
    deep = hidden.shape[1]
    fb = 2 * kb
    cut = pl.BlockSpec((rows, fb), lambda j, _: (0, j))
    half = (rs, zs, ub * kb // wp, wp)
    grad = pl.BlockSpec((rs, 1) + half[2:], lambda j, _: (0, j, 0, 0))
    return call(
        functools.partial(feed_back_body, kb, ub),
        "feed_back",
        (zs,),
        [once(grows.shape), pl.BlockSpec((rs, 2, tall, wp), lambda j, _: (0, j, 0, 0)), cut, cut]
        + [once(gate.shape), once(x_turned.shape), pl.BlockSpec((width, fb), lambda j, _: (0, j))],
        [
            pl.BlockSpec((fb, width), lambda j, _: (j, 0)),
            whole((rows, 128)),
            grad,
            grad,
            whole((rows, width)),
        ],
        [shaped((deep, width), BF16), shaped((rows, 128), F32)]
        + [shaped(half, BF16)] * 2
        + [shaped((rows, width), F32)],
        prefetch=1,
        flops=6 * rows * width * deep,
        nbytes=2 * (3 * width * deep + 2 * rows * deep + 4 * rows * width),
        deps=deps,
    )(bit, grows, w, slope, hidden, gate, x_turned, w_up)


def norm_back(grad, v, inverse, gain):
    scaled = grad * gain
    summed = jnp.sum(scaled * v, axis=-1, keepdims=True)
    return inverse * scaled - v * (inverse * inverse * inverse * summed / v.shape[-1])


def context_back_body(
    kb, nb, bit, total, attn, picked, grows, gate, dots, context, gain, w,
    gmid, gcontext, logit, gsmall, send, keep, gattn, gout,
):
    step = pl.program_id(0)

    @pl.when(step == 0)
    def _():
        gsmall[...] = jnp.zeros_like(gsmall)
        gout[...] = jnp.zeros_like(gout)

    chunk = 128

    def rows_back(i, carry):
        at = pl.ds(pl.multiple_of(i * chunk, chunk), chunk)
        grad = total[at, :]
        rows = picked[at, :].astype(F32)
        middle = rows + attn[at, :]
        inverse = lax.rsqrt(jnp.mean(middle * middle, axis=-1, keepdims=True) + EPSILON)
        gsmall[0:1, :] += jnp.sum(grad * middle * inverse, axis=0, keepdims=True)
        back = norm_back(grad, middle, inverse, gain[...])
        gmid[at, :] = back
        opened, dy = gate[at, :], grows[at, :].astype(F32)
        gattn[at, :] = (opened * dy + back).astype(BF16)
        opening = jnp.sum(dots[at, :], axis=-1, keepdims=True)
        opening += jnp.sum(dy * attn[at, :], axis=-1, keepdims=True)
        opening = opening * opened * (1.0 - opened)
        logit[at, :] = opening
        gsmall[1:2, :] += jnp.sum(opening * rows, axis=0, keepdims=True)
        return carry

    lax.fori_loop(0, total.shape[0] // chunk, rows_back, 0)
    gcontext[...] = mul(gattn[...], w[...], NT).astype(BF16)
    gout[...] += mul(context[...], gattn[...])

    @pl.when(step == pl.num_programs(0) - 1)
    def _():
        grad_cr(bit[0], gout[...].astype(BF16), send, keep, kb, nb)


def context_back(
    bit, total, attn, picked, grows, gate, dots, context, gain, w, shape, wp, steps, deps=()
):
    rows, width = attn.shape
    rs, cs, kb, nb = shape
    half = (rs, cs // 2, kb * nb // wp, wp)
    size = rows // steps
    part = pl.BlockSpec((size, width), lambda j, _: (j, 0))
    thin = pl.BlockSpec((size, 1), lambda j, _: (j, 0))
    return call(
        functools.partial(context_back_body, kb, nb),
        "context_back",
        (steps,),
        [part] * 4
        + [thin, pl.BlockSpec((size, 128), lambda j, _: (j, 0))]
        + [pl.BlockSpec((width, size), lambda j, _: (0, j))]
        + [once(gain.shape), once(w.shape)],
        [part, part, thin, whole((2, width)), whole(half), whole(half)],
        [
            shaped(attn.shape, F32),
            shaped(attn.shape, BF16),
            shaped(gate.shape, F32),
            shaped((2, width), F32),
            shaped(half, BF16),
            shaped(half, BF16),
        ],
        [pltpu.VMEM((size, width), BF16), pltpu.VMEM((width, width), F32)],
        prefetch=1,
        flops=4 * rows * width * width,
        nbytes=26 * rows * width + 6 * width * width,
        deps=deps,
    )(bit, total, attn, picked, grows, gate, dots, context, gain, w)


def attend_back_body(proj, gcontext, probs, out):
    routed = proj.shape[0]
    low, high = halves()
    tiles = [proj[:, i * 2 * HD : (i + 1) * 2 * HD] for i in range(3 * HEADS // 2)]
    grads, weights, grad_probs = [], [], []
    for pair in range(HEADS // 2):
        b, c = tiles[3 * pair + 1], tiles[3 * pair + 2]
        grad = gcontext[:, pair * 2 * HD : (pair + 1) * 2 * HD]
        grads += [grad * low, grad * high]
        for head in (2 * pair, 2 * pair + 1):
            weights.append(probs[0, head * routed : (head + 1) * routed, :])
        grad_probs += [mul(b, grads[-2], NT), mul(c, grads[-1], NT)]
    wide = [weight.astype(F32) for weight in weights]
    inner = [jnp.sum(g * w, axis=0, keepdims=True) for g, w in zip(grad_probs, wide)]
    backs = [(w * (g - i)).astype(BF16) for g, w, i in zip(grad_probs, wide, inner)]
    for pair in range(HEADS // 2):
        a, b, c = (turned(tile) for tile in tiles[3 * pair : 3 * pair + 3])
        (first, second), (low_grad, high_grad) = (
            each[2 * pair : 2 * pair + 2] for each in (backs, grads)
        )
        at = [slice((3 * pair + t) * 2 * HD, (3 * pair + t + 1) * 2 * HD) for t in range(3)]
        out[:, at[0]] = (mul(first, a * low, TN) + mul(first, a * high)).astype(BF16)
        out[:, at[1]] = (mul(weights[2 * pair], low_grad) + mul(second, c * high, TN)).astype(BF16)
        left = jnp.concatenate([second, weights[2 * pair + 1]], axis=1)
        right = jnp.concatenate([b * low, high_grad], axis=0)
        out[:, at[2]] = mul(left, right).astype(BF16)


def attend_back(projected, gcontext, probs, seqs, deps=()):
    rows, wide = projected.shape
    routed = rows // seqs
    return call(
        attend_back_body,
        "attend_back",
        (seqs,),
        [
            pl.BlockSpec((routed, wide), lambda s: (s, 0)),
            pl.BlockSpec((routed, wide // 3), lambda s: (s, 0)),
            pl.BlockSpec((1, HEADS * routed, routed), lambda s: (s, 0, 0)),
        ],
        pl.BlockSpec((routed, wide), lambda s: (s, 0)),
        shaped((rows, wide), BF16),
        flops=40 * rows * wide * routed,
        nbytes=16 * projected.size,
        deps=deps,
    )(projected, gcontext, probs)


def picked_back_body(
    places, gproj, w, logit, gain, router, picked, gmid, grows, base,
    out, total, picked_in, gmid_in, grows_in, fetched, arrived,
):
    j = pl.program_id(0)
    step = w.shape[0]
    loads = [
        pltpu.make_async_copy(source, target, fetched.at[i])
        for i, (source, target) in enumerate(
            ((picked, picked_in), (gmid, gmid_in), (grows, grows_in))
        )
    ]

    @pl.when(j == 0)
    def _():
        for load in loads:
            load.start()

    total[j] = mul(gproj[...], w[...], NT)

    @pl.when(j == pl.num_programs(0) - 1)
    def _():
        for load in loads:
            load.wait()
        chunk = 128
        count = total.shape[1] // chunk

        def compute(i):
            at = pl.ds(pl.multiple_of(i * chunk, chunk), chunk)
            grad = jnp.concatenate([total[n, at, :] for n in range(total.shape[0])], axis=1)
            rows = picked_in[at, :].astype(F32)
            inverse = lax.rsqrt(jnp.mean(rows * rows, axis=-1, keepdims=True) + EPSILON)
            back = norm_back(grad, rows, inverse, gain[...])
            gmid_in[at, :] = (
                gmid_in[at, :]
                + back
                + (logit[at, :] * router[...] + grows_in[at, :].astype(F32))
            )

        def copy(row):
            pltpu.make_async_copy(
                gmid_in.at[pl.ds(row, 1)], out.at[pl.ds(places[row], 1)], arrived
            ).start()

        def both(i, carry):
            for k in range(chunk):
                copy((i - 1) * chunk + k)
            compute(i)
            return carry

        def last(row, carry):
            copy(row)
            return carry

        compute(0)
        lax.fori_loop(1, count, both, 0)
        lax.fori_loop((count - 1) * chunk, count * chunk, last, 0, unroll=8)
        pltpu.make_async_copy(gmid_in, out.at[pl.ds(0, gmid_in.shape[0])], arrived).wait()


def picked_back(places, gproj, w, picked, gmid, logit, grows, gain, router, base, step, deps=()):
    rows, deep = gproj.shape
    width = picked.shape[1]
    return call(
        picked_back_body,
        "picked_back",
        (width // step,),
        [once(gproj.shape), pl.BlockSpec((step, deep), lambda j, _: (j, 0))]
        + [once(t.shape) for t in (logit, gain, router)]
        + [pl.BlockSpec(memory_space=pl.ANY)] * 4,
        pl.BlockSpec(memory_space=pl.ANY),
        shaped(base.shape, F32),
        [
            pltpu.VMEM((width // step, rows, step), F32),
            pltpu.VMEM((rows, width), BF16),
            pltpu.VMEM((rows, width), F32),
            pltpu.VMEM((rows, width), BF16),
            pltpu.SemaphoreType.DMA((3,)),
            pltpu.SemaphoreType.DMA,
        ],
        prefetch=1,
        flops=2 * rows * deep * width,
        nbytes=2 * (gproj.size + w.size) + 10 * picked.size,
        alias={9: 0},
        deps=deps,
    )(places, gproj, w, logit, gain, router, picked, gmid, grows, base)


def join_body(count, *refs):
    out, at = refs[-1], 0
    for keep, got in zip(refs[:count], refs[count : 2 * count]):
        tall = keep.shape[2]

        def add(z, carry):
            total = keep[0, z].astype(F32) + got[0, z].astype(F32)
            out[0, z, at : at + tall, :] = total.astype(BF16)
            return carry

        lax.fori_loop(0, keep.shape[1], add, 0)
        at += tall


def joined(keeps, gots, deps=()):
    rs, zs, _, wp = keeps[0].shape
    talls = [k.shape[2] for k in keeps]
    blocks = [pl.BlockSpec((1, zs, tall, wp), lambda r: (r, 0, 0, 0)) for tall in talls]
    tall = sum(talls)
    return call(
        functools.partial(join_body, len(keeps)),
        "join",
        (rs,),
        blocks * 2,
        pl.BlockSpec((1, zs, tall, wp), lambda r: (r, 0, 0, 0)),
        pltpu.HBM((rs, zs, tall, wp), BF16),
        flops=rs * zs * tall * wp,
        nbytes=6 * rs * zs * tall * wp,
        vmem=40,
        deps=deps,
    )(*[pltpu.with_memory_space_constraint(keep, pltpu.HBM) for keep in keeps], *gots)


def lower_body(hidden, w, attn, picked, gate, kept):
    branch = attn[...] + mul(hidden[...], w[...])
    kept[...] = (picked[...].astype(F32) + gate[...] * branch).astype(BF16)


def lowered(hidden, w, attn, picked, gate, step, deps=()):
    rows, deep = hidden.shape
    width = w.shape[1]
    cut = pl.BlockSpec((rows, step), lambda j: (0, j))
    return call(
        lower_body,
        "lower",
        (width // step,),
        [whole(hidden.shape), pl.BlockSpec((deep, step), lambda j: (0, j))]
        + [cut] * 2
        + [whole(gate.shape)],
        cut,
        shaped((rows, width), BF16),
        flops=2 * rows * deep * width,
        nbytes=2 * (hidden.size + w.size) + 8 * attn.size,
        deps=deps,
    )(hidden, w, attn, picked, gate)


def place_body(index, tok, kept, output):
    found = one_hot(index, tok.shape[0])
    hot = jnp.where(found, 1.0, 0.0)
    routed = jnp.sum(hot, axis=-1, keepdims=True) > 0.5
    output[...] = jnp.where(
        routed, mul(hot.astype(BF16), kept[...]), tok[...].astype(F32)
    ).astype(BF16)


def place(tokens, index, kept, deps=()):
    seqs, _, routed = index.shape
    length, width = tokens.shape[0] // seqs, tokens.shape[1]
    whole_seq = pl.BlockSpec((length, width), lambda s: (s, 0))
    return call(
        place_body,
        "place",
        (seqs,),
        [
            pl.BlockSpec((1, 1, routed), lambda s: (s, 0, 0)),
            whole_seq,
            pl.BlockSpec((routed, width), lambda s: (s, 0)),
        ],
        whole_seq,
        shaped(tokens.shape, BF16),
        flops=2 * seqs * routed * length * width,
        nbytes=4 * tokens.size,
        deps=deps,
    )(index, tokens, kept)


def pieces_body(qkv, out, up, down, small, first, second, third):
    def lay(target, at, block):
        kb, nb = block.shape
        wp = target.shape[1]
        for t in range(nb // wp):
            target[at + t * kb : at + (t + 1) * kb, :] = block[:, t * wp : (t + 1) * wp]

    kb, nb = qkv.shape
    wp = first.shape[1]
    size = kb // 2
    middle = kb * nb // wp // 2
    for t in range(2 * nb // wp):
        at = t * size + (16 if t * size >= middle else 0)
        value = qkv[t % 2 * size : (t % 2 + 1) * size, t // 2 * wp : (t // 2 + 1) * wp]
        first[at : at + size, :] = value
    first[middle : middle + 16, :] = small[...]
    first[2 * middle + 16 :, :] = jnp.zeros_like(small)
    lay(second, 0, up)
    lay(second, up.shape[0] * up.shape[1] // wp, out)
    lay(third, 0, down)


def pieces(qkv, out, up, down, small):
    wp = small.shape[1]
    talls = (qkv.size // wp + 32, (up.size + out.size) // wp, down.size // wp)
    return call(
        pieces_body,
        "pieces",
        (1,),
        [whole(w.shape) for w in (qkv, out, up, down, small)],
        [whole((tall, wp)) for tall in talls],
        [shaped((tall, wp), BF16) for tall in talls],
        nbytes=4 * sum(talls) * wp,
        vmem=60,
    )(qkv, out, up, down, small)


def gathered(flat, rs, cs):
    return lax.all_gather(flat, BOTH, axis=0, tiled=True).reshape(rs, cs, *flat.shape)


def shifted(value, part, shift, rs, cs):
    side = math.isqrt(rs)
    if part == "x":
        moves = [(r, r // side * side + (r + shift) % side) for r in range(rs)]
    elif part == "y":
        moves = [(r, (r + shift * side) % rs) for r in range(rs)]
    else:
        moves = [(c, (c + 2 * shift) % cs) for c in range(cs)]
    return lax.ppermute(value, "col" if part == "z" else "row", moves)


def permuted(flat, rs, cs, during):
    side, zs = math.isqrt(rs), cs // 2
    line = [flat] + [shifted(flat, "z", i, rs, cs) for i in range(1, zs)]
    line[0] = tied(flat, during[0])
    tall = flat.shape[0] // 2
    held = [jnp.stack([part[h * tall : (h + 1) * tall] for part in line])[None] for h in range(2)]
    for order in ("xy", "yx"):
        moved = [
            [shifted(h, part, i, rs, cs) for i in range(1, side)] for h, part in zip(held, order)
        ]
        if order == "xy":
            done, result = during[1](held[0])
        else:
            done, result = during[2](held[0], result)
        held[0] = tied(held[0], done)
        held = [jnp.concatenate([h] + m) for h, m in zip(held, moved)]
    pairs = [(c, c ^ 1) for c in range(cs)]
    return held + [lax.ppermute(h, "col", pairs) for h in held], result


def spots_of(rs, cs):
    side, zs = math.isqrt(rs), cs // 2
    row, column = lax.axis_index("row"), lax.axis_index("col")
    r, z = jnp.arange(rs), jnp.arange(zs)
    y, x = (row // side - r // side) % side, (row - r) % side
    table = jnp.zeros((4, max(rs, zs)), jnp.int32)
    table = table.at[0, :rs].set(y * side + x).at[1, :rs].set(x * side + y)
    return table.at[2, :].set(column % 2).at[3, :zs].set((column // 2 - z) % zs)


def local(
    tokens,
    router_weight,
    norm_first,
    qkv_weight,
    out_weight,
    norm_second,
    up_weight,
    down_weight,
    route_index,
    out_cotangent,
    rs,
    cs,
):
    seqs, routed = route_index.shape
    width = tokens.shape[1]
    index = route_index.reshape(seqs, 1, routed)
    column = lax.axis_index("col")
    core, depth = column % 2, column // 2
    zs = cs // 2
    bit = core.astype(jnp.int32).reshape(1)
    pairs = [(c, c ^ 1) for c in range(cs)]
    blocks = [w.shape for w in (qkv_weight, out_weight, up_weight, down_weight)]
    shape_qkv, shape_out, shape_up, shape_down = ((rs, cs) + b for b in blocks)
    wp = math.gcd(128, *(b[1] for b in blocks))
    tall_qkv, tall_out, tall_up, tall_down = (b[0] * b[1] // wp for b in blocks)

    spots = spots_of(rs, cs)
    small = jnp.concatenate([router_weight, norm_first, norm_second])
    small = jnp.pad(small.reshape(1, -1), ((0, 15), (0, wp - small.shape[0])))
    flat, next_flat, down_flat = pieces(qkv_weight, out_weight, up_weight, down_weight, small)

    def pick_first(dep):
        result = pick("pick_first", out_cotangent, index, True, 0, seqs // 3, deps=(dep,))
        return result[0], result

    def pick_rest(dep, begun):
        result = pick("pick_rest", out_cotangent, index, True, seqs // 3, None, begun, deps=(dep,))
        return result[0], result

    picked = pick("pick", tokens, index, False)
    parts, (grows, base) = permuted(flat, rs, cs, (picked, pick_first, pick_rest))
    next_parts = gathered(next_flat, rs, cs)
    down_parts = gathered(down_flat, rs, cs)

    def exchanged(send):
        return lax.ppermute(send, "col", pairs)

    def by_row(keep):
        r, z, tall, _ = keep.shape
        mine = lax.psum_scatter(
            keep.reshape(r * z * tall, wp), "row", scatter_dimension=0, tiled=True
        )
        return mine.reshape(z, tall, wp)

    def depth_parts(mine):
        return [
            lax.dynamic_index_in_dim(mine, (depth + shift) % zs, 0, keepdims=False)
            for shift in range(zs)
        ]

    def depth_sum(parts, *deps):
        total = (tied(parts[0], *deps) if deps else parts[0]).astype(F32)
        for shift in range(1, zs):
            total = total + shifted(parts[shift], "z", shift, rs, cs).astype(F32)
        return total

    def block(total, shape):
        kb, nb = shape[2:]
        return jnp.concatenate([total[i : i + kb] for i in range(0, kb * nb // wp, kb)], axis=1)

    projected, w_qkv, turned_normed, gmlp, gate, small = project(
        spots, picked, grows, parts, blocks[0][0], blocks[0][1] // wp
    )
    router, first_gain, second_gain = small[0:1], small[1:2], small[2:3]
    context, probs, context_turned = attend(projected, seqs)
    attn, normed_mid, mid_turned, w_out = mix(
        context, next_parts, tall_up // tall_out, tall_out, blocks[1][0], picked, second_gain, 3
    )
    hidden, slope, w_up, down_send, down_keep = raised(
        bit, normed_mid, gmlp, next_parts, 0, tall_up, blocks[2][0], shape_down
    )
    down_keep = joined([down_keep], [exchanged(down_send)])
    down_rows = by_row(down_keep)

    w_down, dots, up_send, up_keep, gnormed = feed_back(
        bit, grows, down_parts, slope, hidden, gate, mid_turned, w_up,
        blocks[3][0], blocks[2][0], deps=(down_keep,),
    )
    up_keep = joined([up_keep], [exchanged(up_send)])
    up_rows = by_row(up_keep)
    gmid, gcontext, logit, gsmall, out_send, out_keep = context_back(
        bit, gnormed, attn, picked, grows, gate, dots, context_turned, second_gain, w_out, shape_out,
        wp, 3, deps=(up_keep,),
    )

    gproj = attend_back(projected, gcontext, probs, seqs)
    qkv_send, gfirst = qkv_weight_grad(
        "qkv_send", bit, turned_normed, gproj, w_qkv, shape_qkv, wp, 2
    )
    qkv_keep, little_send, little_keep = qkv_weight_grad(
        "qkv_keep", bit, turned_normed, gproj, w_qkv, shape_qkv, wp, 2,
        (gsmall, first_gain, gfirst), deps=(qkv_send,),
    )
    qkv_keep = joined(
        [qkv_keep, out_keep, little_keep],
        [exchanged(qkv_send), exchanged(out_send), exchanged(little_send)],
    )
    qkv_rows = by_row(qkv_keep)

    feed_parts = depth_parts(jnp.concatenate([down_rows, up_rows], axis=1))
    starts = jnp.arange(seqs, dtype=jnp.int32) * (tokens.shape[0] // seqs)
    places = (route_index + starts[:, None]).reshape(-1)
    input_grad = picked_back(
        places, gproj, w_qkv, picked, gmid, logit, grows, first_gain, router, base, 256,
        deps=(qkv_keep, *feed_parts),
    )
    kept = lowered(hidden, w_down, attn, picked, gate, 256, deps=(input_grad,))
    feed_total = depth_sum(feed_parts, kept)
    qkv_parts = depth_parts(qkv_rows)
    output = place(tokens, index, kept, deps=(*qkv_parts, feed_total))
    qkv_total = depth_sum(qkv_parts, output)
    down_grad = block(feed_total[:tall_down], shape_down)
    up_grad = block(feed_total[tall_down:], shape_up)
    out_grad = block(qkv_total[tall_qkv : tall_qkv + tall_out], shape_out)
    qkv_grad = block(qkv_total[:tall_qkv], shape_qkv)
    sums = qkv_total[tall_qkv + tall_out, : 3 * width // (rs * cs)].reshape(3, -1)
    return (
        output,
        input_grad,
        sums[1],
        sums[2],
        qkv_grad,
        out_grad,
        sums[0],
        up_grad,
        down_grad,
    )


def solution(mesh):
    both, by_row, by_col = P(BOTH), P("row", "col"), P("col", "row")
    tall = P(BOTH, None)
    return jax.shard_map(
        functools.partial(local, rs=mesh.shape["row"], cs=mesh.shape["col"]),
        mesh=mesh,
        in_specs=(tall, both, both, by_row, by_col, both, by_row, by_col, tall, tall),
        out_specs=(tall, tall, both, both, by_row, by_col, both, by_row, by_col),
        check_vma=False,
    )
```
